512 devices in a mesh: gz: 16 (over y, x_hi, core), ta: 32 (over x_lo, z).
Axes of the slice: x: 4 (x_hi: 2, x_lo: 2; x = x_hi * 2 + x_lo), y: 4, z: 16, core: 2. Of those that a mesh axis runs over, the one named last changes fastest.
Arguments:
- volume: bfloat16 [96, 24, 40, 12288], P('gz', None, None, 'ta'), may hold values from -6 to 6
- sketch_matrix: bfloat16 [12288, 256], P('ta'), may hold values from -0.4375 to 0.4375
- brain_voxels: int32 [57344], P('gz'), may hold values from 0 to 5759, as said below
Outputs:
- sketch: float32 [57344, 256], P(('gz', 'ta'))
The draws below stay inside these ranges and needn't reach their ends.
Inputs may be any that keep to these rules, and one draw needn't show every extreme that they name: `brain_voxels`: each slab's 3584 entries are distinct and increasing; the first is 0 and the last 5759.
All inputs are finite; a program needn't handle non-finite values.
Results may differ from the reference program's by a relative error of at most 0.0003.
Values may be sent and summed in bfloat16 or wider, within the bound.
A program may use at most 64 MiB of HBM per device.

```python
import math
import jax
import jax.numpy as jnp
from jax import lax

RANK = 256
CZ = 6
XW = 24
YW = 40
MASKN = 3584
T_DEV = 384
NZ = 96
TIME = 12288
N_GZ = 16
N_TA = 32


def draw_brain_voxels(key, part):
    slab_cells = CZ * XW * YW

    def single_slab(slab_number):
        slab_key = jax.random.fold_in(key, slab_number)
        shuffled = jax.random.permutation(slab_key, slab_cells - 2) + 1
        chosen = jnp.sort(shuffled[:MASKN - 2]).astype(jnp.int32)
        return jnp.concatenate([jnp.zeros((1,), jnp.int32), chosen, jnp.full((1,), slab_cells - 1, jnp.int32)])
    return jax.vmap(single_slab)(jnp.arange(N_GZ, dtype=jnp.int32)).reshape(-1)


def block_scale(stream_key, shape, split, low, high):
    level = 1.0
    for dim, blocks in split:
        draws = jax.random.uniform(jax.random.fold_in(jax.random.fold_in(stream_key, 6), dim), (blocks,), jnp.float32, low / len(split), high / len(split))
        level = level * jnp.repeat(jnp.exp(draws), shape[dim] // blocks).reshape((-1,) + (1,) * (len(shape) - 1 - dim))
    return level


def bell_draw(rng, shape, width, limit, pieces=(), kind=jnp.bfloat16):
    result = width * jax.random.normal(rng, shape, jnp.float32)
    if pieces:
        result = result * block_scale(rng, shape, pieces, -0.22, 0.18)
    return jnp.clip(result, -limit, limit).astype(kind)


def setup_inputs(seed: int = 0) -> dict:
    key_list = jax.random.split(jax.random.key(seed), 4)
    return {
        "volume": bell_draw(key_list[0], (NZ, XW, YW, TIME), 1.0, 6.0, ((0, 16), (3, 32))),
        "sketch_matrix": bell_draw(key_list[1], (TIME, RANK), (TIME // 64) ** -0.5, 0.4375, ((0, 32),)),
        "brain_voxels": draw_brain_voxels(jax.random.fold_in(key_list[3], 71), 0),
    }


def kernel_taps():
    sigma = 3.0 / (2.0 * math.sqrt(2.0 * math.log(2.0)))
    raw_taps = [math.exp(-0.5 * (shift_k - 2) ** 2 / sigma ** 2) for shift_k in range(5)]
    summed = sum(raw_taps)
    return [value_k / summed for value_k in raw_taps]

def smooth_along(source, axis_num, kernel):
    extent = source.shape[axis_num]
    widths = [(0, 0)] * source.ndim
    widths[axis_num] = (2, 2)
    padded = jnp.pad(source, widths)
    summed = jnp.zeros_like(source)
    for shift_k in range(5):
        summed = summed + kernel[shift_k] * lax.slice_in_dim(padded, shift_k, shift_k + extent, axis=axis_num)
    return summed

def reference(volume, sketch_matrix, brain_voxels):
    kernel = kernel_taps()
    slab_cells = CZ * XW * YW
    offsets = (jnp.arange(N_GZ, dtype=jnp.int32) * slab_cells)[:, None]
    row_index = (brain_voxels.reshape(N_GZ, MASKN) + offsets).reshape(-1)

    def time_block(step_index, summed):
        first_col = (step_index * T_DEV).astype(jnp.int32)
        signal = lax.dynamic_slice_in_dim(volume, first_col, T_DEV, axis=3).astype(jnp.float32)
        for axis_num in (0, 1, 2):
            signal = smooth_along(signal, axis_num, kernel)
        picked = signal.reshape(NZ * XW * YW, T_DEV)[row_index]
        weights = lax.dynamic_slice_in_dim(sketch_matrix, first_col, T_DEV, axis=0).astype(jnp.float32)
        return summed + jnp.dot(picked, weights, precision=lax.Precision.HIGHEST, preferred_element_type=jnp.float32)
    start_sum = jnp.zeros((N_GZ * MASKN, RANK), jnp.float32)
    return lax.fori_loop(0, N_TA, time_block, start_sum)
```

```python
import functools
import math

import jax
import jax.numpy as jnp
from jax import lax
from jax.experimental import pallas as pl
from jax.experimental.pallas import tpu as pltpu
from jax.sharding import PartitionSpec as P

MESH = pl.DeviceIdType.MESH
Z_RING = 16


def with_halo(shard, sides, width):
    for axis, dim in sides:
        peers, length = (lax.axis_size(axis), shard.shape[dim])
        up = [(i, (i + 1) % peers) for i in range(peers - 1)]
        down = [(j, i) for i, j in up]
        last = lax.slice_in_dim(shard, length - width, length, axis=dim)
        initial = lax.slice_in_dim(shard, 0, width, axis=dim)
        before = lax.ppermute(last, axis, up)
        after = lax.ppermute(initial, axis, down)
        shard = jnp.concatenate([before, shard, after], axis=dim)
    return shard


def kernel_taps():
    sigma = 3.0 / (2.0 * math.sqrt(2.0 * math.log(2.0)))
    raw_taps = [math.exp(-0.5 * (shift_k - 2) ** 2 / sigma**2) for shift_k in range(5)]
    summed = sum(raw_taps)
    return [value_k / summed for value_k in raw_taps]


def smooth_along(source, axis_num, kernel):
    extent = source.shape[axis_num]
    widths = [(0, 0)] * source.ndim
    widths[axis_num] = (2, 2)
    padded = jnp.pad(source, widths)
    summed = jnp.zeros_like(source)
    for shift_k in range(5):
        summed = summed + kernel[shift_k] * lax.slice_in_dim(
            padded, shift_k, shift_k + extent, axis=axis_num
        )
    return summed


def smooth_planes(padded, planes, kernel):
    summed = kernel[0] * padded[0:planes].astype(jnp.float32)
    for shift_k in range(1, 5):
        summed = summed + kernel[shift_k] * padded[shift_k : shift_k + planes].astype(jnp.float32)
    return summed


def rs_kernel(nz, p_ref, o_ref, recv, send, fin, xrecv, send_sem, recv_sem, credit, xsem):
    gz = lax.axis_index("gz")
    ta = lax.axis_index("ta")
    xl = ta // nz
    zi = ta % nz
    right = xl * nz + (zi + 1) % nz
    left = xl * nz + (zi + nz - 1) % nz
    partner = (1 - xl) * nz + zi

    barrier = pltpu.get_barrier_semaphore()
    for peer in (left, right, partner):
        pl.semaphore_signal(barrier, 1, device_id=(gz, peer), device_id_type=MESH)
    pl.semaphore_wait(barrier, 3)

    dirs = (
        (0, right, left, lambda s: (zi + 2 * nz - s - 1) % nz),
        (1, left, right, lambda s: nz + (zi + s + 1) % nz),
    )
    copies = {}
    for s in range(nz):
        for d, dst, src_peer, chunk in dirs:
            blk = chunk(s)
            if s == 0:
                src = p_ref.at[blk]
            else:
                copies[(d, s - 1)].wait_recv()
                val = recv[d, (s - 1) % 2] + p_ref[blk]
                if s < nz - 1:
                    if s >= 2:
                        copies[(d, s - 2)].wait_send()
                    send[d, s % 2] = val
                    src = send.at[d, s % 2]
                    if s <= nz - 3:
                        pl.semaphore_signal(credit.at[d], 1, device_id=(gz, src_peer), device_id_type=MESH)
                else:
                    fin[d] = val
            if s < nz - 1:
                if s >= 2:
                    pl.semaphore_wait(credit.at[d], 1)
                cp = pltpu.make_async_remote_copy(
                    src_ref=src,
                    dst_ref=recv.at[d, s % 2],
                    send_sem=send_sem.at[d, s % 2],
                    recv_sem=recv_sem.at[d, s % 2],
                    device_id=(gz, dst),
                    device_id_type=MESH,
                )
                cp.start()
                copies[(d, s)] = cp

    xcp = pltpu.make_async_remote_copy(
        src_ref=fin.at[1 - xl],
        dst_ref=xrecv,
        send_sem=xsem.at[0],
        recv_sem=xsem.at[1],
        device_id=(gz, partner),
        device_id_type=MESH,
    )
    xcp.start()
    for d in range(2):
        for s in (nz - 3, nz - 2):
            copies[(d, s)].wait_send()
    xcp.wait_recv()
    o_ref[...] = fin[xl] + xrecv[...]
    xcp.wait_send()


def reduce_scatter_ta(partial, n_ta):
    rows_all, cols = partial.shape
    nz = Z_RING
    assert n_ta == 2 * nz
    rows = rows_all // n_ta
    blocks = partial.reshape(n_ta, rows, cols)
    return pl.pallas_call(
        functools.partial(rs_kernel, nz),
        out_shape=jax.ShapeDtypeStruct((rows, cols), jnp.float32),
        in_specs=[pl.BlockSpec(memory_space=pltpu.VMEM)],
        out_specs=pl.BlockSpec(memory_space=pltpu.VMEM),
        scratch_shapes=[
            pltpu.VMEM((2, 2, rows, cols), jnp.float32),
            pltpu.VMEM((2, 2, rows, cols), jnp.float32),
            pltpu.VMEM((2, rows, cols), jnp.float32),
            pltpu.VMEM((rows, cols), jnp.float32),
            pltpu.SemaphoreType.DMA((2, 2)),
            pltpu.SemaphoreType.DMA((2, 2)),
            pltpu.SemaphoreType.REGULAR((2,)),
            pltpu.SemaphoreType.DMA((2,)),
        ],
        compiler_params=pltpu.CompilerParams(collective_id=0, has_side_effects=True),
    )(blocks)


def shards(volume, sketch_matrix, brain_voxels):
    kernel = kernel_taps()
    planes, width_x, width_y, time_local = volume.shape
    slab_cells = planes * width_x * width_y
    weights = sketch_matrix.astype(jnp.float32)
    padded = with_halo(volume, (("gz", 0),), 2)
    signal = smooth_planes(padded, planes, kernel)
    signal = smooth_along(signal, 1, kernel)
    signal = smooth_along(signal, 2, kernel)
    picked = signal.reshape(slab_cells, time_local)[brain_voxels]
    partial = jnp.dot(
        picked, weights, precision=lax.Precision.HIGHEST, preferred_element_type=jnp.float32
    )
    return reduce_scatter_ta(partial, lax.axis_size("ta"))


def solution(mesh):
    in_specs = (P("gz", None, None, "ta"), P("ta", None), P("gz"))
    out_specs = P(("gz", "ta"), None)
    return jax.shard_map(shards, mesh=mesh, in_specs=in_specs, out_specs=out_specs, check_vma=False)
```

```python
import functools
import math

import jax
import jax.numpy as jnp
from jax import lax
from jax.experimental import pallas as pl
from jax.experimental.pallas import tpu as pltpu
from jax.sharding import PartitionSpec as P

MESH = pl.DeviceIdType.MESH
Z_RING = 16


def with_halo(shard, sides, width):
    for axis, dim in sides:
        peers, length = (lax.axis_size(axis), shard.shape[dim])
        up = [(i, (i + 1) % peers) for i in range(peers - 1)]
        down = [(j, i) for i, j in up]
        last = lax.slice_in_dim(shard, length - width, length, axis=dim)
        initial = lax.slice_in_dim(shard, 0, width, axis=dim)
        before = lax.ppermute(last, axis, up)
        after = lax.ppermute(initial, axis, down)
        shard = jnp.concatenate([before, shard, after], axis=dim)
    return shard


def kernel_taps():
    sigma = 3.0 / (2.0 * math.sqrt(2.0 * math.log(2.0)))
    raw_taps = [math.exp(-0.5 * (shift_k - 2) ** 2 / sigma**2) for shift_k in range(5)]
    summed = sum(raw_taps)
    return [value_k / summed for value_k in raw_taps]


def smooth_along(source, axis_num, kernel):
    extent = source.shape[axis_num]
    widths = [(0, 0)] * source.ndim
    widths[axis_num] = (2, 2)
    padded = jnp.pad(source, widths)
    summed = jnp.zeros_like(source)
    for shift_k in range(5):
        summed = summed + kernel[shift_k] * lax.slice_in_dim(
            padded, shift_k, shift_k + extent, axis=axis_num
        )
    return summed


def smooth_planes(padded, planes, kernel):
    summed = kernel[0] * padded[0:planes].astype(jnp.float32)
    for shift_k in range(1, 5):
        summed = summed + kernel[shift_k] * padded[shift_k : shift_k + planes].astype(jnp.float32)
    return summed


def rs_kernel(nz, p_ref, o_ref, recv, send, fin, xrecv, send_sem, recv_sem, credit, xsem):
    gz = lax.axis_index("gz")
    ta = lax.axis_index("ta")
    xl = ta // nz
    zi = ta % nz
    right = xl * nz + (zi + 1) % nz
    left = xl * nz + (zi + nz - 1) % nz
    partner = (1 - xl) * nz + zi

    barrier = pltpu.get_barrier_semaphore()
    for peer in (left, right, partner):
        pl.semaphore_signal(barrier, 1, device_id=(gz, peer), device_id_type=MESH)
    pl.semaphore_wait(barrier, 3)

    dirs = (
        (0, right, left, lambda s: (zi + 2 * nz - s - 1) % nz),
        (1, left, right, lambda s: nz + (zi + s + 1) % nz),
    )
    copies = {}
    for s in range(nz):
        for d, dst, src_peer, chunk in dirs:
            blk = chunk(s)
            if s == 0:
                src = p_ref.at[blk]
            else:
                copies[(d, s - 1)].wait_recv()
                val = recv[d, (s - 1) % 2] + p_ref[blk]
                if s < nz - 1:
                    if s >= 2:
                        copies[(d, s - 2)].wait_send()
                    send[d, s % 2] = val
                    src = send.at[d, s % 2]
                    if s <= nz - 3:
                        pl.semaphore_signal(credit.at[d], 1, device_id=(gz, src_peer), device_id_type=MESH)
                else:
                    fin[d] = val
            if s < nz - 1:
                if s >= 2:
                    pl.semaphore_wait(credit.at[d], 1)
                cp = pltpu.make_async_remote_copy(
                    src_ref=src,
                    dst_ref=recv.at[d, s % 2],
                    send_sem=send_sem.at[d, s % 2],
                    recv_sem=recv_sem.at[d, s % 2],
                    device_id=(gz, dst),
                    device_id_type=MESH,
                )
                cp.start()
                copies[(d, s)] = cp

    xcp = pltpu.make_async_remote_copy(
        src_ref=fin.at[1 - xl],
        dst_ref=xrecv,
        send_sem=xsem.at[0],
        recv_sem=xsem.at[1],
        device_id=(gz, partner),
        device_id_type=MESH,
    )
    xcp.start()
    for d in range(2):
        for s in (nz - 3, nz - 2):
            copies[(d, s)].wait_send()
    xcp.wait_recv()
    o_ref[...] = fin[xl] + xrecv[...]
    xcp.wait_send()


def reduce_scatter_ta(partial, n_ta):
    rows_all, cols = partial.shape
    nz = Z_RING
    assert n_ta == 2 * nz
    rows = rows_all // n_ta
    blocks = partial.reshape(n_ta, rows, cols)
    return pl.pallas_call(
        functools.partial(rs_kernel, nz),
        out_shape=jax.ShapeDtypeStruct((rows, cols), jnp.float32),
        in_specs=[pl.BlockSpec(memory_space=pltpu.VMEM)],
        out_specs=pl.BlockSpec(memory_space=pltpu.VMEM),
        scratch_shapes=[
            pltpu.VMEM((2, 2, rows, cols), jnp.float32),
            pltpu.VMEM((2, 2, rows, cols), jnp.float32),
            pltpu.VMEM((2, rows, cols), jnp.float32),
            pltpu.VMEM((rows, cols), jnp.float32),
            pltpu.SemaphoreType.DMA((2, 2)),
            pltpu.SemaphoreType.DMA((2, 2)),
            pltpu.SemaphoreType.REGULAR((2,)),
            pltpu.SemaphoreType.DMA((2,)),
        ],
        compiler_params=pltpu.CompilerParams(collective_id=0, has_side_effects=True),
    )(blocks)


def shards(volume, sketch_matrix, brain_voxels):
    kernel = kernel_taps()
    planes, width_x, width_y, time_local = volume.shape
    slab_cells = planes * width_x * width_y
    rank = sketch_matrix.shape[1]
    padded = with_halo(volume, (("gz", 0),), 2)
    projected = jnp.dot(
        padded.reshape(-1, time_local), sketch_matrix, preferred_element_type=jnp.float32
    ).reshape(planes + 4, width_x, width_y, rank)
    signal = smooth_planes(projected, planes, kernel)
    signal = smooth_along(signal, 1, kernel)
    signal = smooth_along(signal, 2, kernel)
    partial = signal.reshape(slab_cells, rank)[brain_voxels]
    return reduce_scatter_ta(partial, lax.axis_size("ta"))


def solution(mesh):
    in_specs = (P("gz", None, None, "ta"), P("ta", None), P("gz"))
    out_specs = P(("gz", "ta"), None)
    return jax.shard_map(shards, mesh=mesh, in_specs=in_specs, out_specs=out_specs, check_vma=False)
```

```python
import functools
import math

import jax
import jax.numpy as jnp
from jax import lax
from jax.experimental import pallas as pl
from jax.experimental.pallas import tpu as pltpu
from jax.sharding import PartitionSpec as P

MESH = pl.DeviceIdType.MESH
Z_RING = 16


def with_halo(shard, sides, width):
    for axis, dim in sides:
        peers, length = (lax.axis_size(axis), shard.shape[dim])
        up = [(i, (i + 1) % peers) for i in range(peers - 1)]
        down = [(j, i) for i, j in up]
        last = lax.slice_in_dim(shard, length - width, length, axis=dim)
        initial = lax.slice_in_dim(shard, 0, width, axis=dim)
        before = lax.ppermute(last, axis, up)
        after = lax.ppermute(initial, axis, down)
        shard = jnp.concatenate([before, shard, after], axis=dim)
    return shard


def kernel_taps():
    sigma = 3.0 / (2.0 * math.sqrt(2.0 * math.log(2.0)))
    raw_taps = [math.exp(-0.5 * (shift_k - 2) ** 2 / sigma**2) for shift_k in range(5)]
    summed = sum(raw_taps)
    return [value_k / summed for value_k in raw_taps]


def smooth_along(source, axis_num, kernel):
    extent = source.shape[axis_num]
    widths = [(0, 0)] * source.ndim
    widths[axis_num] = (2, 2)
    padded = jnp.pad(source, widths)
    summed = jnp.zeros_like(source)
    for shift_k in range(5):
        summed = summed + kernel[shift_k] * lax.slice_in_dim(
            padded, shift_k, shift_k + extent, axis=axis_num
        )
    return summed


def smooth_planes(padded, planes, kernel):
    summed = kernel[0] * padded[0:planes].astype(jnp.float32)
    for shift_k in range(1, 5):
        summed = summed + kernel[shift_k] * padded[shift_k : shift_k + planes].astype(jnp.float32)
    return summed


def rs_kernel(nz, parts, p_ref, o_ref, recv, send, fin, xrecv, send_sem, recv_sem, credit, xsem):
    gz = lax.axis_index("gz")
    ta = lax.axis_index("ta")
    xl = ta // nz
    zi = ta % nz
    right = xl * nz + (zi + 1) % nz
    left = xl * nz + (zi + nz - 1) % nz
    partner = (1 - xl) * nz + zi
    rk = recv.shape[3]

    barrier = pltpu.get_barrier_semaphore()
    for peer in (left, right, partner):
        pl.semaphore_signal(barrier, 1, device_id=(gz, peer), device_id_type=MESH)
    pl.semaphore_wait(barrier, 3)

    dirs = (
        (0, right, left, lambda s: (zi + 2 * nz - s - 1) % nz),
        (1, left, right, lambda s: nz + (zi + s + 1) % nz),
    )
    copies = {}
    for s in range(nz):
        for k in range(parts):
            for d, dst, src_peer, chunk in dirs:
                blk = chunk(s)
                own = p_ref.at[blk, pl.ds(k * rk, rk)]
                if s == 0:
                    src = own
                else:
                    copies[(d, k, s - 1)].wait_recv()
                    val = recv[d, k, (s - 1) % 2] + own[...]
                    if s < nz - 1:
                        if s >= 2:
                            copies[(d, k, s - 2)].wait_send()
                        send[d, k, s % 2] = val
                        src = send.at[d, k, s % 2]
                        if s <= nz - 3:
                            pl.semaphore_signal(
                                credit.at[d, k], 1, device_id=(gz, src_peer), device_id_type=MESH
                            )
                    else:
                        fin[d, pl.ds(k * rk, rk)] = val
                if s < nz - 1:
                    if s >= 2:
                        pl.semaphore_wait(credit.at[d, k], 1)
                    cp = pltpu.make_async_remote_copy(
                        src_ref=src,
                        dst_ref=recv.at[d, k, s % 2],
                        send_sem=send_sem.at[d, k, s % 2],
                        recv_sem=recv_sem.at[d, k, s % 2],
                        device_id=(gz, dst),
                        device_id_type=MESH,
                    )
                    cp.start()
                    copies[(d, k, s)] = cp

    xcp = pltpu.make_async_remote_copy(
        src_ref=fin.at[1 - xl],
        dst_ref=xrecv,
        send_sem=xsem.at[0],
        recv_sem=xsem.at[1],
        device_id=(gz, partner),
        device_id_type=MESH,
    )
    xcp.start()
    for d in range(2):
        for k in range(parts):
            for s in (nz - 3, nz - 2):
                copies[(d, k, s)].wait_send()
    xcp.wait_recv()
    o_ref[...] = fin[xl] + xrecv[...]
    xcp.wait_send()


def reduce_scatter_ta(partial, n_ta, parts=2):
    rows_all, cols = partial.shape
    nz = Z_RING
    assert n_ta == 2 * nz
    rows = rows_all // n_ta
    rk = rows // parts
    blocks = partial.reshape(n_ta, rows, cols)
    return pl.pallas_call(
        functools.partial(rs_kernel, nz, parts),
        out_shape=jax.ShapeDtypeStruct((rows, cols), jnp.float32),
        in_specs=[pl.BlockSpec(memory_space=pltpu.VMEM)],
        out_specs=pl.BlockSpec(memory_space=pltpu.VMEM),
        scratch_shapes=[
            pltpu.VMEM((2, parts, 2, rk, cols), jnp.float32),
            pltpu.VMEM((2, parts, 2, rk, cols), jnp.float32),
            pltpu.VMEM((2, rows, cols), jnp.float32),
            pltpu.VMEM((rows, cols), jnp.float32),
            pltpu.SemaphoreType.DMA((2, parts, 2)),
            pltpu.SemaphoreType.DMA((2, parts, 2)),
            pltpu.SemaphoreType.REGULAR((2, parts)),
            pltpu.SemaphoreType.DMA((2,)),
        ],
        compiler_params=pltpu.CompilerParams(collective_id=0, has_side_effects=True),
    )(blocks)


def shards(volume, sketch_matrix, brain_voxels):
    kernel = kernel_taps()
    planes, width_x, width_y, time_local = volume.shape
    slab_cells = planes * width_x * width_y
    rank = sketch_matrix.shape[1]
    padded = with_halo(volume, (("gz", 0),), 2)
    projected = jnp.dot(
        padded.reshape(-1, time_local), sketch_matrix, preferred_element_type=jnp.float32
    ).reshape(planes + 4, width_x, width_y, rank)
    signal = smooth_planes(projected, planes, kernel)
    signal = smooth_along(signal, 1, kernel)
    signal = smooth_along(signal, 2, kernel)
    partial = signal.reshape(slab_cells, rank)[brain_voxels]
    return reduce_scatter_ta(partial, lax.axis_size("ta"))


def solution(mesh):
    in_specs = (P("gz", None, None, "ta"), P("ta", None), P("gz"))
    out_specs = P(("gz", "ta"), None)
    return jax.shard_map(shards, mesh=mesh, in_specs=in_specs, out_specs=out_specs, check_vma=False)
```

```python
import functools
import math

import jax
import jax.numpy as jnp
from jax import lax
from jax.experimental import pallas as pl
from jax.experimental.pallas import tpu as pltpu
from jax.sharding import PartitionSpec as P

MESH = pl.DeviceIdType.MESH
Z_RING = 16


def kernel_taps():
    sigma = 3.0 / (2.0 * math.sqrt(2.0 * math.log(2.0)))
    raw_taps = [math.exp(-0.5 * (shift_k - 2) ** 2 / sigma**2) for shift_k in range(5)]
    summed = sum(raw_taps)
    return [value_k / summed for value_k in raw_taps]


def smooth_along(source, axis_num, kernel):
    extent = source.shape[axis_num]
    widths = [(0, 0)] * source.ndim
    widths[axis_num] = (2, 2)
    padded = jnp.pad(source, widths)
    summed = jnp.zeros_like(source)
    for shift_k in range(5):
        summed = summed + kernel[shift_k] * lax.slice_in_dim(
            padded, shift_k, shift_k + extent, axis=axis_num
        )
    return summed


def smooth_planes(padded, planes, kernel):
    summed = kernel[0] * padded[0:planes].astype(jnp.float32)
    for shift_k in range(1, 5):
        summed = summed + kernel[shift_k] * padded[shift_k : shift_k + planes].astype(jnp.float32)
    return summed


def rs_kernel(nz, parts, p_ref, o_ref, recv, send, fin, xrecv, send_sem, recv_sem, credit, xsem):
    gz = lax.axis_index("gz")
    ta = lax.axis_index("ta")
    xl = ta // nz
    zi = ta % nz
    right = xl * nz + (zi + 1) % nz
    left = xl * nz + (zi + nz - 1) % nz
    partner = (1 - xl) * nz + zi
    rk = recv.shape[3]

    barrier = pltpu.get_barrier_semaphore()
    for peer in (left, right, partner):
        pl.semaphore_signal(barrier, 1, device_id=(gz, peer), device_id_type=MESH)
    pl.semaphore_wait(barrier, 3)

    dirs = (
        (0, right, left, lambda s: (zi + 2 * nz - s - 1) % nz),
        (1, left, right, lambda s: nz + (zi + s + 1) % nz),
    )
    copies = {}
    for s in range(nz):
        for k in range(parts):
            for d, dst, src_peer, chunk in dirs:
                blk = chunk(s)
                own = p_ref.at[blk, pl.ds(k * rk, rk)]
                if s == 0:
                    src = own
                else:
                    copies[(d, k, s - 1)].wait_recv()
                    val = recv[d, k, (s - 1) % 2] + own[...]
                    if s < nz - 1:
                        if s >= 2:
                            copies[(d, k, s - 2)].wait_send()
                        send[d, k, s % 2] = val
                        src = send.at[d, k, s % 2]
                        if s <= nz - 3:
                            pl.semaphore_signal(
                                credit.at[d, k], 1, device_id=(gz, src_peer), device_id_type=MESH
                            )
                    else:
                        fin[d, pl.ds(k * rk, rk)] = val
                if s < nz - 1:
                    if s >= 2:
                        pl.semaphore_wait(credit.at[d, k], 1)
                    cp = pltpu.make_async_remote_copy(
                        src_ref=src,
                        dst_ref=recv.at[d, k, s % 2],
                        send_sem=send_sem.at[d, k, s % 2],
                        recv_sem=recv_sem.at[d, k, s % 2],
                        device_id=(gz, dst),
                        device_id_type=MESH,
                    )
                    cp.start()
                    copies[(d, k, s)] = cp

    xcp = pltpu.make_async_remote_copy(
        src_ref=fin.at[1 - xl],
        dst_ref=xrecv,
        send_sem=xsem.at[0],
        recv_sem=xsem.at[1],
        device_id=(gz, partner),
        device_id_type=MESH,
    )
    xcp.start()
    for d in range(2):
        for k in range(parts):
            for s in (nz - 3, nz - 2):
                copies[(d, k, s)].wait_send()
    xcp.wait_recv()
    o_ref[...] = fin[xl] + xrecv[...]
    xcp.wait_send()


def reduce_scatter_ta(partial, n_ta, parts=2):
    rows_all, cols = partial.shape
    nz = Z_RING
    assert n_ta == 2 * nz
    rows = rows_all // n_ta
    rk = rows // parts
    blocks = partial.reshape(n_ta, rows, cols)
    return pl.pallas_call(
        functools.partial(rs_kernel, nz, parts),
        out_shape=jax.ShapeDtypeStruct((rows, cols), jnp.float32),
        in_specs=[pl.BlockSpec(memory_space=pltpu.VMEM)],
        out_specs=pl.BlockSpec(memory_space=pltpu.VMEM),
        scratch_shapes=[
            pltpu.VMEM((2, parts, 2, rk, cols), jnp.float32),
            pltpu.VMEM((2, parts, 2, rk, cols), jnp.float32),
            pltpu.VMEM((2, rows, cols), jnp.float32),
            pltpu.VMEM((rows, cols), jnp.float32),
            pltpu.SemaphoreType.DMA((2, parts, 2)),
            pltpu.SemaphoreType.DMA((2, parts, 2)),
            pltpu.SemaphoreType.REGULAR((2, parts)),
            pltpu.SemaphoreType.DMA((2,)),
        ],
        compiler_params=pltpu.CompilerParams(collective_id=0, has_side_effects=True),
    )(blocks)


def exchange_halo(shard, axis, width):
    peers, length = lax.axis_size(axis), shard.shape[0]
    up = [(i, i + 1) for i in range(peers - 1)]
    down = [(j, i) for i, j in up]
    below = lax.ppermute(shard[length - width :], axis, up)
    above = lax.ppermute(shard[:width], axis, down)
    return below, above


def project_smooth_xy(planes_bf16, sketch_matrix, kernel):
    count, width_x, width_y, time_local = planes_bf16.shape
    projected = jnp.dot(
        planes_bf16.reshape(-1, time_local), sketch_matrix, preferred_element_type=jnp.float32
    ).reshape(count, width_x, width_y, sketch_matrix.shape[1])
    return smooth_along(smooth_along(projected, 1, kernel), 2, kernel)


def shards(volume, sketch_matrix, brain_voxels):
    kernel = kernel_taps()
    planes, width_x, width_y, time_local = volume.shape
    slab_cells = planes * width_x * width_y
    rank = sketch_matrix.shape[1]
    below, above = exchange_halo(volume, "gz", 2)
    local = project_smooth_xy(volume, sketch_matrix, kernel)
    halo = project_smooth_xy(jnp.concatenate([below, above]), sketch_matrix, kernel)
    padded = jnp.concatenate([halo[:2], local, halo[2:]])
    signal = smooth_planes(padded, planes, kernel)
    partial = signal.reshape(slab_cells, rank)[brain_voxels]
    return reduce_scatter_ta(partial, lax.axis_size("ta"))


def solution(mesh):
    in_specs = (P("gz", None, None, "ta"), P("ta", None), P("gz"))
    out_specs = P(("gz", "ta"), None)
    return jax.shard_map(shards, mesh=mesh, in_specs=in_specs, out_specs=out_specs, check_vma=False)
```

```python
import functools
import math

import jax
import jax.numpy as jnp
from jax import lax
from jax.experimental import pallas as pl
from jax.experimental.pallas import tpu as pltpu
from jax.sharding import PartitionSpec as P

MESH = pl.DeviceIdType.MESH
Z_RING = 16


def kernel_taps():
    sigma = 3.0 / (2.0 * math.sqrt(2.0 * math.log(2.0)))
    raw_taps = [math.exp(-0.5 * (shift_k - 2) ** 2 / sigma**2) for shift_k in range(5)]
    summed = sum(raw_taps)
    return [value_k / summed for value_k in raw_taps]


def smooth_along(source, axis_num, kernel):
    extent = source.shape[axis_num]
    widths = [(0, 0)] * source.ndim
    widths[axis_num] = (2, 2)
    padded = jnp.pad(source, widths)
    summed = jnp.zeros_like(source)
    for shift_k in range(5):
        summed = summed + kernel[shift_k] * lax.slice_in_dim(
            padded, shift_k, shift_k + extent, axis=axis_num
        )
    return summed


def smooth_planes(padded, planes, kernel):
    summed = kernel[0] * padded[0:planes].astype(jnp.float32)
    for shift_k in range(1, 5):
        summed = summed + kernel[shift_k] * padded[shift_k : shift_k + planes].astype(jnp.float32)
    return summed


def rs_kernel(nz, parts, p_ref, o_ref, recv, send, fin, xrecv, send_sem, recv_sem, credit, xsem):
    gz = lax.axis_index("gz")
    ta = lax.axis_index("ta")
    xl = ta // nz
    zi = ta % nz
    right = xl * nz + (zi + 1) % nz
    left = xl * nz + (zi + nz - 1) % nz
    partner = (1 - xl) * nz + zi
    rk = recv.shape[3]

    barrier = pltpu.get_barrier_semaphore()
    for peer in (left, right, partner):
        pl.semaphore_signal(barrier, 1, device_id=(gz, peer), device_id_type=MESH)
    pl.semaphore_wait(barrier, 3)

    dirs = (
        (0, right, left, lambda s: (zi + 2 * nz - s - 1) % nz),
        (1, left, right, lambda s: nz + (zi + s + 1) % nz),
    )
    copies = {}
    for s in range(nz):
        for k in range(parts):
            for d, dst, src_peer, chunk in dirs:
                blk = chunk(s)
                own = p_ref.at[blk, pl.ds(k * rk, rk)]
                if s == 0:
                    src = own
                else:
                    copies[(d, k, s - 1)].wait_recv()
                    val = recv[d, k, (s - 1) % 2] + own[...]
                    if s < nz - 1:
                        if s >= 2:
                            copies[(d, k, s - 2)].wait_send()
                        send[d, k, s % 2] = val
                        src = send.at[d, k, s % 2]
                        if s <= nz - 3:
                            pl.semaphore_signal(
                                credit.at[d, k], 1, device_id=(gz, src_peer), device_id_type=MESH
                            )
                    else:
                        fin[d, pl.ds(k * rk, rk)] = val
                if s < nz - 1:
                    if s >= 2:
                        pl.semaphore_wait(credit.at[d, k], 1)
                    cp = pltpu.make_async_remote_copy(
                        src_ref=src,
                        dst_ref=recv.at[d, k, s % 2],
                        send_sem=send_sem.at[d, k, s % 2],
                        recv_sem=recv_sem.at[d, k, s % 2],
                        device_id=(gz, dst),
                        device_id_type=MESH,
                    )
                    cp.start()
                    copies[(d, k, s)] = cp

    xcp = pltpu.make_async_remote_copy(
        src_ref=fin.at[1 - xl],
        dst_ref=xrecv,
        send_sem=xsem.at[0],
        recv_sem=xsem.at[1],
        device_id=(gz, partner),
        device_id_type=MESH,
    )
    xcp.start()
    for d in range(2):
        for k in range(parts):
            for s in (nz - 3, nz - 2):
                copies[(d, k, s)].wait_send()
    xcp.wait_recv()
    o_ref[...] = fin[xl] + xrecv[...]
    xcp.wait_send()


def reduce_scatter_ta(partial, n_ta, parts=7):
    rows_all, cols = partial.shape
    nz = Z_RING
    assert n_ta == 2 * nz
    rows = rows_all // n_ta
    rk = rows // parts
    blocks = partial.reshape(n_ta, rows, cols)
    return pl.pallas_call(
        functools.partial(rs_kernel, nz, parts),
        out_shape=jax.ShapeDtypeStruct((rows, cols), jnp.float32),
        in_specs=[pl.BlockSpec(memory_space=pltpu.VMEM)],
        out_specs=pl.BlockSpec(memory_space=pltpu.VMEM),
        scratch_shapes=[
            pltpu.VMEM((2, parts, 2, rk, cols), jnp.float32),
            pltpu.VMEM((2, parts, 2, rk, cols), jnp.float32),
            pltpu.VMEM((2, rows, cols), jnp.float32),
            pltpu.VMEM((rows, cols), jnp.float32),
            pltpu.SemaphoreType.DMA((2, parts, 2)),
            pltpu.SemaphoreType.DMA((2, parts, 2)),
            pltpu.SemaphoreType.REGULAR((2, parts)),
            pltpu.SemaphoreType.DMA((2,)),
        ],
        compiler_params=pltpu.CompilerParams(collective_id=0, has_side_effects=True),
    )(blocks)


def exchange_halo(shard, axis, width):
    peers, length = lax.axis_size(axis), shard.shape[0]
    up = [(i, i + 1) for i in range(peers - 1)]
    down = [(j, i) for i, j in up]
    below = lax.ppermute(shard[length - width :], axis, up)
    above = lax.ppermute(shard[:width], axis, down)
    return below, above


def project_smooth_xy(planes_bf16, sketch_matrix, kernel):
    count, width_x, width_y, time_local = planes_bf16.shape
    projected = jnp.dot(
        planes_bf16.reshape(-1, time_local), sketch_matrix, preferred_element_type=jnp.float32
    ).reshape(count, width_x, width_y, sketch_matrix.shape[1])
    return smooth_along(smooth_along(projected, 1, kernel), 2, kernel)


def shards(volume, sketch_matrix, brain_voxels):
    kernel = kernel_taps()
    planes, width_x, width_y, time_local = volume.shape
    slab_cells = planes * width_x * width_y
    rank = sketch_matrix.shape[1]
    below, above = exchange_halo(volume, "gz", 2)
    local = project_smooth_xy(volume, sketch_matrix, kernel)
    halo = project_smooth_xy(jnp.concatenate([below, above]), sketch_matrix, kernel)
    padded = jnp.concatenate([halo[:2], local, halo[2:]])
    signal = smooth_planes(padded, planes, kernel)
    partial = signal.reshape(slab_cells, rank)[brain_voxels]
    return reduce_scatter_ta(partial, lax.axis_size("ta"))


def solution(mesh):
    in_specs = (P("gz", None, None, "ta"), P("ta", None), P("gz"))
    out_specs = P(("gz", "ta"), None)
    return jax.shard_map(shards, mesh=mesh, in_specs=in_specs, out_specs=out_specs, check_vma=False)
```

```python
import functools
import math

import jax
import jax.numpy as jnp
from jax import lax
from jax.experimental import pallas as pl
from jax.experimental.pallas import tpu as pltpu
from jax.sharding import PartitionSpec as P

MESH = pl.DeviceIdType.MESH
Z_RING = 16


def kernel_taps():
    sigma = 3.0 / (2.0 * math.sqrt(2.0 * math.log(2.0)))
    raw_taps = [math.exp(-0.5 * (shift_k - 2) ** 2 / sigma**2) for shift_k in range(5)]
    summed = sum(raw_taps)
    return [value_k / summed for value_k in raw_taps]


def smooth_along(source, axis_num, kernel):
    extent = source.shape[axis_num]
    widths = [(0, 0)] * source.ndim
    widths[axis_num] = (2, 2)
    padded = jnp.pad(source, widths)
    summed = jnp.zeros_like(source)
    for shift_k in range(5):
        summed = summed + kernel[shift_k] * lax.slice_in_dim(
            padded, shift_k, shift_k + extent, axis=axis_num
        )
    return summed


def smooth_planes(padded, planes, kernel):
    summed = kernel[0] * padded[0:planes].astype(jnp.float32)
    for shift_k in range(1, 5):
        summed = summed + kernel[shift_k] * padded[shift_k : shift_k + planes].astype(jnp.float32)
    return summed


def rs_kernel(nz, parts, p_ref, o_ref, recv, send, fin, xrecv, send_sem, recv_sem, credit, xsem):
    gz = lax.axis_index("gz")
    ta = lax.axis_index("ta")
    xl = ta // nz
    zi = ta % nz
    right = xl * nz + (zi + 1) % nz
    left = xl * nz + (zi + nz - 1) % nz
    partner = (1 - xl) * nz + zi
    rk = recv.shape[3]

    barrier = pltpu.get_barrier_semaphore()
    for peer in (left, right, partner):
        pl.semaphore_signal(barrier, 1, device_id=(gz, peer), device_id_type=MESH)
    pl.semaphore_wait(barrier, 3)

    dirs = (
        (0, right, left, lambda s: (zi + 2 * nz - s - 1) % nz),
        (1, left, right, lambda s: nz + (zi + s + 1) % nz),
    )
    copies = {}
    for s in range(nz):
        for k in range(parts):
            for d, dst, src_peer, chunk in dirs:
                blk = chunk(s)
                own = p_ref.at[blk, pl.ds(k * rk, rk)]
                if s == 0:
                    src = own
                else:
                    copies[(d, k, s - 1)].wait_recv()
                    val = recv[d, k, (s - 1) % 2] + own[...]
                    if s < nz - 1:
                        if s >= 2:
                            copies[(d, k, s - 2)].wait_send()
                        send[d, k, s % 2] = val
                        src = send.at[d, k, s % 2]
                        if s <= nz - 3:
                            pl.semaphore_signal(
                                credit.at[d, k], 1, device_id=(gz, src_peer), device_id_type=MESH
                            )
                    else:
                        fin[d, pl.ds(k * rk, rk)] = val
                if s < nz - 1:
                    if s >= 2:
                        pl.semaphore_wait(credit.at[d, k], 1)
                    cp = pltpu.make_async_remote_copy(
                        src_ref=src,
                        dst_ref=recv.at[d, k, s % 2],
                        send_sem=send_sem.at[d, k, s % 2],
                        recv_sem=recv_sem.at[d, k, s % 2],
                        device_id=(gz, dst),
                        device_id_type=MESH,
                    )
                    cp.start()
                    copies[(d, k, s)] = cp

    xcp = pltpu.make_async_remote_copy(
        src_ref=fin.at[1 - xl],
        dst_ref=xrecv,
        send_sem=xsem.at[0],
        recv_sem=xsem.at[1],
        device_id=(gz, partner),
        device_id_type=MESH,
    )
    xcp.start()
    for d in range(2):
        for k in range(parts):
            for s in (nz - 3, nz - 2):
                copies[(d, k, s)].wait_send()
    xcp.wait_recv()
    o_ref[...] = fin[xl] + xrecv[...]
    xcp.wait_send()


def reduce_scatter_ta(partial, n_ta, parts=7):
    rows_all, cols = partial.shape
    nz = Z_RING
    assert n_ta == 2 * nz
    rows = rows_all // n_ta
    rk = rows // parts
    blocks = partial.reshape(n_ta, rows, cols)
    return pl.pallas_call(
        functools.partial(rs_kernel, nz, parts),
        out_shape=jax.ShapeDtypeStruct((rows, cols), jnp.float32),
        in_specs=[pl.BlockSpec(memory_space=pltpu.VMEM)],
        out_specs=pl.BlockSpec(memory_space=pltpu.VMEM),
        scratch_shapes=[
            pltpu.VMEM((2, parts, 2, rk, cols), jnp.float32),
            pltpu.VMEM((2, parts, 2, rk, cols), jnp.float32),
            pltpu.VMEM((2, rows, cols), jnp.float32),
            pltpu.VMEM((rows, cols), jnp.float32),
            pltpu.SemaphoreType.DMA((2, parts, 2)),
            pltpu.SemaphoreType.DMA((2, parts, 2)),
            pltpu.SemaphoreType.REGULAR((2, parts)),
            pltpu.SemaphoreType.DMA((2,)),
        ],
        compiler_params=pltpu.CompilerParams(collective_id=0, has_side_effects=True),
    )(blocks)


Y_SIZE, X_SIZE = 4, 4


def _coords(lin, n_ta):
    gz, ta = divmod(lin, n_ta)
    y, x_hi, core = gz // 4, (gz // 2) % 2, gz % 2
    x_lo, z = divmod(ta, Z_RING)
    return y, x_hi * 2 + x_lo, z, core


def _lin(y, x, z, core, n_ta):
    gz = (y * 2 + x // 2) * 2 + core
    return gz * n_ta + (x % 2) * Z_RING + z


def halo_routes(n_gz, n_ta):
    onchip, first, second = [], ([], []), ([], [])
    for lin in range(n_gz * n_ta):
        gz = lin // n_ta
        y, x, z, core = _coords(lin, n_ta)
        onchip.append((lin, _lin(y, x, z, 1 - core, n_ta)))
        dest_gz = gz + 1 if core == 1 else gz - 1
        if not 0 <= dest_gz < n_gz:
            continue
        dest = dest_gz * n_ta + lin % n_ta
        for half, step in enumerate((1, -1)):
            relay = _lin(y, (x + step) % X_SIZE, z, core, n_ta)
            first[half].append((lin, relay))
            second[half].append((relay, dest))
    return onchip, first, second


def exchange_halo(shard, width):
    n_gz, n_ta = lax.axis_size("gz"), lax.axis_size("ta")
    onchip, first, second = halo_routes(n_gz, n_ta)
    axes = ("gz", "ta")
    core = lax.axis_index("gz") % 2
    length, width_x = shard.shape[0], shard.shape[1]
    top, bottom = shard[length - width :], shard[:width]
    near = lax.ppermute(jnp.where(core == 0, top, bottom), axes, onchip)
    far_out = jnp.where(core == 1, top, bottom)
    cut = width_x // 2
    halves = (far_out[:, :cut], far_out[:, cut:])
    relayed = [lax.ppermute(h, axes, p) for h, p in zip(halves, first)]
    far = jnp.concatenate([lax.ppermute(h, axes, p) for h, p in zip(relayed, second)], axis=1)
    below = jnp.where(core == 0, far, near)
    above = jnp.where(core == 0, near, far)
    return below, above


def project_smooth_xy(planes_bf16, sketch_matrix, kernel):
    count, width_x, width_y, time_local = planes_bf16.shape
    projected = jnp.dot(
        planes_bf16.reshape(-1, time_local), sketch_matrix, preferred_element_type=jnp.float32
    ).reshape(count, width_x, width_y, sketch_matrix.shape[1])
    return smooth_along(smooth_along(projected, 1, kernel), 2, kernel)


def shards(volume, sketch_matrix, brain_voxels):
    kernel = kernel_taps()
    planes, width_x, width_y, time_local = volume.shape
    slab_cells = planes * width_x * width_y
    rank = sketch_matrix.shape[1]
    below, above = exchange_halo(volume, 2)
    local = project_smooth_xy(volume, sketch_matrix, kernel)
    halo = project_smooth_xy(jnp.concatenate([below, above]), sketch_matrix, kernel)
    padded = jnp.concatenate([halo[:2], local, halo[2:]])
    signal = smooth_planes(padded, planes, kernel)
    partial = signal.reshape(slab_cells, rank)[brain_voxels]
    return reduce_scatter_ta(partial, lax.axis_size("ta"))


def solution(mesh):
    in_specs = (P("gz", None, None, "ta"), P("ta", None), P("gz"))
    out_specs = P(("gz", "ta"), None)
    return jax.shard_map(shards, mesh=mesh, in_specs=in_specs, out_specs=out_specs, check_vma=False)
```

```python
import functools
import math

import jax
import jax.numpy as jnp
from jax import lax
from jax.experimental import pallas as pl
from jax.experimental.pallas import tpu as pltpu
from jax.sharding import PartitionSpec as P

MESH = pl.DeviceIdType.MESH
Z_RING = 16


def kernel_taps():
    sigma = 3.0 / (2.0 * math.sqrt(2.0 * math.log(2.0)))
    raw_taps = [math.exp(-0.5 * (shift_k - 2) ** 2 / sigma**2) for shift_k in range(5)]
    summed = sum(raw_taps)
    return [value_k / summed for value_k in raw_taps]


def smooth_along(source, axis_num, kernel):
    extent = source.shape[axis_num]
    widths = [(0, 0)] * source.ndim
    widths[axis_num] = (2, 2)
    padded = jnp.pad(source, widths)
    summed = jnp.zeros_like(source)
    for shift_k in range(5):
        summed = summed + kernel[shift_k] * lax.slice_in_dim(
            padded, shift_k, shift_k + extent, axis=axis_num
        )
    return summed


def smooth_planes(padded, planes, kernel):
    summed = kernel[0] * padded[0:planes].astype(jnp.float32)
    for shift_k in range(1, 5):
        summed = summed + kernel[shift_k] * padded[shift_k : shift_k + planes].astype(jnp.float32)
    return summed


def rs_kernel(nz, parts, p_ref, o_ref, recv, send, fin, xrecv, send_sem, recv_sem, credit, xsem):
    gz = lax.axis_index("gz")
    ta = lax.axis_index("ta")
    xl = ta // nz
    zi = ta % nz
    right = xl * nz + (zi + 1) % nz
    left = xl * nz + (zi + nz - 1) % nz
    partner = (1 - xl) * nz + zi
    rk = recv.shape[3]

    barrier = pltpu.get_barrier_semaphore()
    for peer in (left, right, partner):
        pl.semaphore_signal(barrier, 1, device_id=(gz, peer), device_id_type=MESH)
    pl.semaphore_wait(barrier, 3)

    dirs = (
        (0, right, left, lambda s: (zi + 2 * nz - s - 1) % nz),
        (1, left, right, lambda s: nz + (zi + s + 1) % nz),
    )
    copies = {}
    for s in range(nz):
        for k in range(parts):
            for d, dst, src_peer, chunk in dirs:
                blk = chunk(s)
                own = p_ref.at[blk, pl.ds(k * rk, rk)]
                if s == 0:
                    src = own
                else:
                    copies[(d, k, s - 1)].wait_recv()
                    val = recv[d, k, (s - 1) % 2] + own[...]
                    if s < nz - 1:
                        if s >= 2:
                            copies[(d, k, s - 2)].wait_send()
                        send[d, k, s % 2] = val
                        src = send.at[d, k, s % 2]
                        if s <= nz - 3:
                            pl.semaphore_signal(
                                credit.at[d, k], 1, device_id=(gz, src_peer), device_id_type=MESH
                            )
                    else:
                        fin[d, pl.ds(k * rk, rk)] = val
                if s < nz - 1:
                    if s >= 2:
                        pl.semaphore_wait(credit.at[d, k], 1)
                    cp = pltpu.make_async_remote_copy(
                        src_ref=src,
                        dst_ref=recv.at[d, k, s % 2],
                        send_sem=send_sem.at[d, k, s % 2],
                        recv_sem=recv_sem.at[d, k, s % 2],
                        device_id=(gz, dst),
                        device_id_type=MESH,
                    )
                    cp.start()
                    copies[(d, k, s)] = cp
            if s == nz - 1:
                xcp = pltpu.make_async_remote_copy(
                    src_ref=fin.at[1 - xl, pl.ds(k * rk, rk)],
                    dst_ref=xrecv.at[pl.ds(k * rk, rk)],
                    send_sem=xsem.at[0, k],
                    recv_sem=xsem.at[1, k],
                    device_id=(gz, partner),
                    device_id_type=MESH,
                )
                xcp.start()
                copies[("x", k)] = xcp

    for d in range(2):
        for k in range(parts):
            for s in (nz - 3, nz - 2):
                copies[(d, k, s)].wait_send()
    for k in range(parts):
        copies[("x", k)].wait_recv()
    o_ref[...] = fin[xl] + xrecv[...]
    for k in range(parts):
        copies[("x", k)].wait_send()


def reduce_scatter_ta(partial, n_ta, parts=14):
    rows_all, cols = partial.shape
    nz = Z_RING
    assert n_ta == 2 * nz
    rows = rows_all // n_ta
    rk = rows // parts
    blocks = partial.reshape(n_ta, rows, cols)
    return pl.pallas_call(
        functools.partial(rs_kernel, nz, parts),
        out_shape=jax.ShapeDtypeStruct((rows, cols), jnp.float32),
        in_specs=[pl.BlockSpec(memory_space=pltpu.VMEM)],
        out_specs=pl.BlockSpec(memory_space=pltpu.VMEM),
        scratch_shapes=[
            pltpu.VMEM((2, parts, 2, rk, cols), jnp.float32),
            pltpu.VMEM((2, parts, 2, rk, cols), jnp.float32),
            pltpu.VMEM((2, rows, cols), jnp.float32),
            pltpu.VMEM((rows, cols), jnp.float32),
            pltpu.SemaphoreType.DMA((2, parts, 2)),
            pltpu.SemaphoreType.DMA((2, parts, 2)),
            pltpu.SemaphoreType.REGULAR((2, parts)),
            pltpu.SemaphoreType.DMA((2, parts)),
        ],
        compiler_params=pltpu.CompilerParams(collective_id=0, has_side_effects=True),
    )(blocks)


def exchange_halo(shard, axis, width):
    peers, length = lax.axis_size(axis), shard.shape[0]
    up = [(i, i + 1) for i in range(peers - 1)]
    down = [(j, i) for i, j in up]
    below = lax.ppermute(shard[length - width :], axis, up)
    above = lax.ppermute(shard[:width], axis, down)
    return below, above


def project_smooth_xy(planes_bf16, sketch_matrix, kernel):
    count, width_x, width_y, time_local = planes_bf16.shape
    projected = jnp.dot(
        planes_bf16.reshape(-1, time_local), sketch_matrix, preferred_element_type=jnp.float32
    ).reshape(count, width_x, width_y, sketch_matrix.shape[1])
    return smooth_along(smooth_along(projected, 1, kernel), 2, kernel)


def shards(volume, sketch_matrix, brain_voxels):
    kernel = kernel_taps()
    planes, width_x, width_y, time_local = volume.shape
    slab_cells = planes * width_x * width_y
    rank = sketch_matrix.shape[1]
    below, above = exchange_halo(volume, "gz", 2)
    local = project_smooth_xy(volume, sketch_matrix, kernel)
    halo = project_smooth_xy(jnp.concatenate([below, above]), sketch_matrix, kernel)
    padded = jnp.concatenate([halo[:2], local, halo[2:]])
    signal = smooth_planes(padded, planes, kernel)
    partial = signal.reshape(slab_cells, rank)[brain_voxels]
    return reduce_scatter_ta(partial, lax.axis_size("ta"))


def solution(mesh):
    in_specs = (P("gz", None, None, "ta"), P("ta", None), P("gz"))
    out_specs = P(("gz", "ta"), None)
    return jax.shard_map(shards, mesh=mesh, in_specs=in_specs, out_specs=out_specs, check_vma=False)
```

```python
import functools
import math

import jax
import jax.numpy as jnp
from jax import lax
from jax.experimental import pallas as pl
from jax.experimental.pallas import tpu as pltpu
from jax.sharding import PartitionSpec as P

MESH = pl.DeviceIdType.MESH
Z_RING = 16


def kernel_taps():
    sigma = 3.0 / (2.0 * math.sqrt(2.0 * math.log(2.0)))
    raw_taps = [math.exp(-0.5 * (shift_k - 2) ** 2 / sigma**2) for shift_k in range(5)]
    summed = sum(raw_taps)
    return [value_k / summed for value_k in raw_taps]


def smooth_along(source, axis_num, kernel):
    extent = source.shape[axis_num]
    widths = [(0, 0)] * source.ndim
    widths[axis_num] = (2, 2)
    padded = jnp.pad(source, widths)
    summed = jnp.zeros_like(source)
    for shift_k in range(5):
        summed = summed + kernel[shift_k] * lax.slice_in_dim(
            padded, shift_k, shift_k + extent, axis=axis_num
        )
    return summed


def smooth_planes(padded, planes, kernel):
    summed = kernel[0] * padded[0:planes].astype(jnp.float32)
    for shift_k in range(1, 5):
        summed = summed + kernel[shift_k] * padded[shift_k : shift_k + planes].astype(jnp.float32)
    return summed


def rs_kernel(nz, parts, p_ref, o_ref, recv, send, fin, xrecv, send_sem, recv_sem, credit, xsem):
    gz = lax.axis_index("gz")
    ta = lax.axis_index("ta")
    xl = ta // nz
    zi = ta % nz
    right = xl * nz + (zi + 1) % nz
    left = xl * nz + (zi + nz - 1) % nz
    partner = (1 - xl) * nz + zi
    rk = recv.shape[3]

    barrier = pltpu.get_barrier_semaphore()
    for peer in (left, right, partner):
        pl.semaphore_signal(barrier, 1, device_id=(gz, peer), device_id_type=MESH)
    pl.semaphore_wait(barrier, 3)

    dirs = (
        (0, right, left, lambda s: (zi + 2 * nz - s - 1) % nz),
        (1, left, right, lambda s: nz + (zi + s + 1) % nz),
    )
    copies = {}
    for s in range(nz):
        for k in range(parts):
            for d, dst, src_peer, chunk in dirs:
                blk = chunk(s)
                own = p_ref.at[blk, pl.ds(k * rk, rk)]
                if s == 0:
                    src = own
                else:
                    copies[(d, k, s - 1)].wait_recv()
                    val = recv[d, k, (s - 1) % 2] + own[...]
                    if s < nz - 1:
                        if s >= 2:
                            copies[(d, k, s - 2)].wait_send()
                        send[d, k, s % 2] = val
                        src = send.at[d, k, s % 2]
                        if s <= nz - 3:
                            pl.semaphore_signal(
                                credit.at[d, k], 1, device_id=(gz, src_peer), device_id_type=MESH
                            )
                    else:
                        fin[d, pl.ds(k * rk, rk)] = val
                if s < nz - 1:
                    if s >= 2:
                        pl.semaphore_wait(credit.at[d, k], 1)
                    cp = pltpu.make_async_remote_copy(
                        src_ref=src,
                        dst_ref=recv.at[d, k, s % 2],
                        send_sem=send_sem.at[d, k, s % 2],
                        recv_sem=recv_sem.at[d, k, s % 2],
                        device_id=(gz, dst),
                        device_id_type=MESH,
                    )
                    cp.start()
                    copies[(d, k, s)] = cp
            if s == nz - 1:
                xcp = pltpu.make_async_remote_copy(
                    src_ref=fin.at[1 - xl, pl.ds(k * rk, rk)],
                    dst_ref=xrecv.at[pl.ds(k * rk, rk)],
                    send_sem=xsem.at[0, k],
                    recv_sem=xsem.at[1, k],
                    device_id=(gz, partner),
                    device_id_type=MESH,
                )
                xcp.start()
                copies[("x", k)] = xcp

    for d in range(2):
        for k in range(parts):
            for s in (nz - 3, nz - 2):
                copies[(d, k, s)].wait_send()
    for k in range(parts):
        copies[("x", k)].wait_recv()
    o_ref[...] = fin[xl] + xrecv[...]
    for k in range(parts):
        copies[("x", k)].wait_send()


def reduce_scatter_ta(partial, n_ta, parts=14):
    rows_all, cols = partial.shape
    nz = Z_RING
    assert n_ta == 2 * nz
    rows = rows_all // n_ta
    rk = rows // parts
    blocks = partial.reshape(n_ta, rows, cols)
    return pl.pallas_call(
        functools.partial(rs_kernel, nz, parts),
        out_shape=jax.ShapeDtypeStruct((rows, cols), jnp.float32),
        in_specs=[pl.BlockSpec(memory_space=pltpu.VMEM)],
        out_specs=pl.BlockSpec(memory_space=pltpu.VMEM),
        scratch_shapes=[
            pltpu.VMEM((2, parts, 2, rk, cols), jnp.float32),
            pltpu.VMEM((2, parts, 2, rk, cols), jnp.float32),
            pltpu.VMEM((2, rows, cols), jnp.float32),
            pltpu.VMEM((rows, cols), jnp.float32),
            pltpu.SemaphoreType.DMA((2, parts, 2)),
            pltpu.SemaphoreType.DMA((2, parts, 2)),
            pltpu.SemaphoreType.REGULAR((2, parts)),
            pltpu.SemaphoreType.DMA((2, parts)),
        ],
        compiler_params=pltpu.CompilerParams(collective_id=0, has_side_effects=True),
    )(blocks)


def halo_kernel(nz, n_gz, vol_ref, o_ref, relay, halo, sems):
    gz = lax.axis_index("gz")
    ta = lax.axis_index("ta")
    length, width_x = vol_ref.shape[0], vol_ref.shape[1]
    width = halo.shape[1]
    cut = width_x // 2
    y, core = gz // 4, gz % 2
    x = ((gz // 2) % 2) * 2 + ta // nz
    zi = ta % nz

    def dev(yy, xx):
        return ((yy * 2 + xx // 2) * 2 + core, (xx % 2) * nz + zi)

    def flows(g):
        return jnp.logical_or(
            jnp.logical_and(core == 1, g < n_gz - 1), jnp.logical_and(core == 0, g > 0)
        )

    step = 2 * core - 1
    partner = (gz - step, ta)
    near = ((y, (x + 1) % 4), (y, (x + 3) % 4))
    sources = (dev(*near[1]), dev(*near[0]))
    src_gz = gz + step
    has_src = jnp.logical_and(src_gz >= 0, src_gz < n_gz)
    src_y, src_x = src_gz // 4, ((src_gz // 2) % 2) * 2 + ta // nz
    src_relays = (
        (src_y, (src_x + 1) % 4),
        (src_y, (src_x + 3) % 4),
    )

    barrier = pltpu.get_barrier_semaphore()

    def signal(target):
        pl.semaphore_signal(barrier, 1, device_id=target, device_id_type=MESH)

    signal(partner)
    for rel in near:
        signal(dev(*rel))
    relays_for = []
    for h in range(2):
        s_gz, s_ta = sources[h]
        live = flows(s_gz)
        relays_for.append(live)
        pl.when(live)(functools.partial(signal, (s_gz + step, s_ta)))
    for h in range(2):
        ry, rx = src_relays[h]
        pl.when(has_src)(functools.partial(signal, ((ry * 2 + rx // 2) * 2 + (1 - core), (rx % 2) * nz + zi)))
    count = 3 + relays_for[0].astype(jnp.int32) + relays_for[1].astype(jnp.int32) + 2 * has_src.astype(jnp.int32)
    pl.semaphore_wait(barrier, count)

    def copy(src, dst, i, target):
        return pltpu.make_async_remote_copy(
            src_ref=src, dst_ref=dst, send_sem=sems.at[0, i], recv_sem=sems.at[1, i],
            device_id=target, device_id_type=MESH,
        )

    near_copy = copy(vol_ref.at[pl.ds((1 - core) * (length - width), width)], halo.at[core], 0, partner)
    near_copy.start()
    mine = flows(gz)
    first = [
        copy(vol_ref.at[pl.ds(core * (length - width), width), pl.ds(h * cut, cut)], relay.at[h], 1 + h,
             dev(*near[h]))
        for h in range(2)
    ]
    second = [
        copy(relay.at[h], halo.at[1 - core, :, pl.ds(h * cut, cut)], 3 + h,
             (sources[h][0] + step, sources[h][1]))
        for h in range(2)
    ]

    @pl.when(mine)
    def _():
        for h in range(2):
            first[h].start()

    for h in range(2):
        @pl.when(relays_for[h])
        def _():
            first[h].wait_recv()
            second[h].start()

    @pl.when(jnp.logical_not(has_src))
    def _():
        halo[core] = jnp.zeros(halo.shape[1:], halo.dtype)

    near_copy.wait_recv()
    near_copy.wait_send()

    @pl.when(has_src)
    def _():
        for h in range(2):
            second[h].wait_recv()

    @pl.when(mine)
    def _():
        for h in range(2):
            first[h].wait_send()

    for h in range(2):
        @pl.when(relays_for[h])
        def _():
            second[h].wait_send()

    o_ref[...] = halo[...]


def exchange_halo(shard, width, nz=Z_RING):
    length, width_x, width_y, time_local = shard.shape
    halo = pl.pallas_call(
        functools.partial(halo_kernel, nz, lax.axis_size("gz")),
        out_shape=jax.ShapeDtypeStruct((2, width, width_x, width_y, time_local), shard.dtype),
        in_specs=[pl.BlockSpec(memory_space=pltpu.VMEM)],
        out_specs=pl.BlockSpec(memory_space=pltpu.VMEM),
        scratch_shapes=[
            pltpu.VMEM((2, width, width_x // 2, width_y, time_local), shard.dtype),
            pltpu.VMEM((2, width, width_x, width_y, time_local), shard.dtype),
            pltpu.SemaphoreType.DMA((2, 5)),
        ],
        compiler_params=pltpu.CompilerParams(collective_id=1, has_side_effects=True),
    )(shard)
    return halo[0], halo[1]


def project_smooth_xy(planes_bf16, sketch_matrix, kernel):
    count, width_x, width_y, time_local = planes_bf16.shape
    projected = jnp.dot(
        planes_bf16.reshape(-1, time_local), sketch_matrix, preferred_element_type=jnp.float32
    ).reshape(count, width_x, width_y, sketch_matrix.shape[1])
    return smooth_along(smooth_along(projected, 1, kernel), 2, kernel)


def shards(volume, sketch_matrix, brain_voxels):
    kernel = kernel_taps()
    planes, width_x, width_y, time_local = volume.shape
    slab_cells = planes * width_x * width_y
    rank = sketch_matrix.shape[1]
    below, above = exchange_halo(volume, 2)
    local = project_smooth_xy(volume, sketch_matrix, kernel)
    halo = project_smooth_xy(jnp.concatenate([below, above]), sketch_matrix, kernel)
    padded = jnp.concatenate([halo[:2], local, halo[2:]])
    signal = smooth_planes(padded, planes, kernel)
    partial = signal.reshape(slab_cells, rank)[brain_voxels]
    return reduce_scatter_ta(partial, lax.axis_size("ta"))


def solution(mesh):
    in_specs = (P("gz", None, None, "ta"), P("ta", None), P("gz"))
    out_specs = P(("gz", "ta"), None)
    return jax.shard_map(shards, mesh=mesh, in_specs=in_specs, out_specs=out_specs, check_vma=False)
```

```python
import functools
import math

import jax
import jax.numpy as jnp
from jax import lax
from jax.experimental import pallas as pl
from jax.experimental.pallas import tpu as pltpu
from jax.sharding import PartitionSpec as P

MESH = pl.DeviceIdType.MESH
Z_RING = 16
SLOTS = 3


def kernel_taps():
    sigma = 3.0 / (2.0 * math.sqrt(2.0 * math.log(2.0)))
    raw_taps = [math.exp(-0.5 * (shift_k - 2) ** 2 / sigma**2) for shift_k in range(5)]
    summed = sum(raw_taps)
    return [value_k / summed for value_k in raw_taps]


def smooth_along(source, axis_num, kernel):
    extent = source.shape[axis_num]
    widths = [(0, 0)] * source.ndim
    widths[axis_num] = (2, 2)
    padded = jnp.pad(source, widths)
    summed = jnp.zeros_like(source)
    for shift_k in range(5):
        summed = summed + kernel[shift_k] * lax.slice_in_dim(
            padded, shift_k, shift_k + extent, axis=axis_num
        )
    return summed


def smooth_planes(padded, planes, kernel):
    summed = kernel[0] * padded[0:planes].astype(jnp.float32)
    for shift_k in range(1, 5):
        summed = summed + kernel[shift_k] * padded[shift_k : shift_k + planes].astype(jnp.float32)
    return summed


def rs_kernel(nz, parts, p_ref, o_ref, recv, send, fin, xrecv, send_sem, recv_sem, credit, xsem):
    gz = lax.axis_index("gz")
    ta = lax.axis_index("ta")
    xl = ta // nz
    zi = ta % nz
    right = xl * nz + (zi + 1) % nz
    left = xl * nz + (zi + nz - 1) % nz
    partner = (1 - xl) * nz + zi
    rk = recv.shape[3]

    barrier = pltpu.get_barrier_semaphore()
    for peer in (left, right, partner):
        pl.semaphore_signal(barrier, 1, device_id=(gz, peer), device_id_type=MESH)
    pl.semaphore_wait(barrier, 3)

    dirs = (
        (0, right, left, lambda s: (zi + 2 * nz - s - 1) % nz),
        (1, left, right, lambda s: nz + (zi + s + 1) % nz),
    )
    copies = {}
    for s in range(nz):
        for k in range(parts):
            for d, dst, src_peer, chunk in dirs:
                blk = chunk(s)
                own = p_ref.at[blk, pl.ds(k * rk, rk)]
                if s == 0:
                    src = own
                else:
                    copies[(d, k, s - 1)].wait_recv()
                    val = recv[d, k, (s - 1) % SLOTS] + own[...]
                    if s < nz - 1:
                        if s >= SLOTS:
                            copies[(d, k, s - SLOTS)].wait_send()
                        send[d, k, s % SLOTS] = val
                        src = send.at[d, k, s % SLOTS]
                        if s <= nz - 1 - SLOTS:
                            pl.semaphore_signal(
                                credit.at[d, k], 1, device_id=(gz, src_peer), device_id_type=MESH
                            )
                    else:
                        fin[d, pl.ds(k * rk, rk)] = val
                if s < nz - 1:
                    if s >= SLOTS:
                        pl.semaphore_wait(credit.at[d, k], 1)
                    cp = pltpu.make_async_remote_copy(
                        src_ref=src,
                        dst_ref=recv.at[d, k, s % SLOTS],
                        send_sem=send_sem.at[d, k, s % SLOTS],
                        recv_sem=recv_sem.at[d, k, s % SLOTS],
                        device_id=(gz, dst),
                        device_id_type=MESH,
                    )
                    cp.start()
                    copies[(d, k, s)] = cp
            if s == nz - 1:
                xcp = pltpu.make_async_remote_copy(
                    src_ref=fin.at[1 - xl, pl.ds(k * rk, rk)],
                    dst_ref=xrecv.at[pl.ds(k * rk, rk)],
                    send_sem=xsem.at[0, k],
                    recv_sem=xsem.at[1, k],
                    device_id=(gz, partner),
                    device_id_type=MESH,
                )
                xcp.start()
                copies[("x", k)] = xcp

    for d in range(2):
        for k in range(parts):
            for s in range(nz - 1 - SLOTS, nz - 1):
                copies[(d, k, s)].wait_send()
    for k in range(parts):
        copies[("x", k)].wait_recv()
    o_ref[...] = fin[xl] + xrecv[...]
    for k in range(parts):
        copies[("x", k)].wait_send()


def reduce_scatter_ta(partial, n_ta, parts=14):
    rows_all, cols = partial.shape
    nz = Z_RING
    assert n_ta == 2 * nz
    rows = rows_all // n_ta
    rk = rows // parts
    blocks = partial.reshape(n_ta, rows, cols)
    return pl.pallas_call(
        functools.partial(rs_kernel, nz, parts),
        out_shape=jax.ShapeDtypeStruct((rows, cols), jnp.float32),
        in_specs=[pl.BlockSpec(memory_space=pltpu.VMEM)],
        out_specs=pl.BlockSpec(memory_space=pltpu.VMEM),
        scratch_shapes=[
            pltpu.VMEM((2, parts, SLOTS, rk, cols), jnp.float32),
            pltpu.VMEM((2, parts, SLOTS, rk, cols), jnp.float32),
            pltpu.VMEM((2, rows, cols), jnp.float32),
            pltpu.VMEM((rows, cols), jnp.float32),
            pltpu.SemaphoreType.DMA((2, parts, SLOTS)),
            pltpu.SemaphoreType.DMA((2, parts, SLOTS)),
            pltpu.SemaphoreType.REGULAR((2, parts)),
            pltpu.SemaphoreType.DMA((2, parts)),
        ],
        compiler_params=pltpu.CompilerParams(collective_id=0, has_side_effects=True),
    )(blocks)


def exchange_halo(shard, axis, width):
    peers, length = lax.axis_size(axis), shard.shape[0]
    up = [(i, i + 1) for i in range(peers - 1)]
    down = [(j, i) for i, j in up]
    below = lax.ppermute(shard[length - width :], axis, up)
    above = lax.ppermute(shard[:width], axis, down)
    return below, above


def project_smooth_xy(planes_bf16, sketch_matrix, kernel):
    count, width_x, width_y, time_local = planes_bf16.shape
    projected = jnp.dot(
        planes_bf16.reshape(-1, time_local), sketch_matrix, preferred_element_type=jnp.float32
    ).reshape(count, width_x, width_y, sketch_matrix.shape[1])
    return smooth_along(smooth_along(projected, 1, kernel), 2, kernel)


def shards(volume, sketch_matrix, brain_voxels):
    kernel = kernel_taps()
    planes, width_x, width_y, time_local = volume.shape
    slab_cells = planes * width_x * width_y
    rank = sketch_matrix.shape[1]
    below, above = exchange_halo(volume, "gz", 2)
    local = project_smooth_xy(volume, sketch_matrix, kernel)
    halo = project_smooth_xy(jnp.concatenate([below, above]), sketch_matrix, kernel)
    padded = jnp.concatenate([halo[:2], local, halo[2:]])
    signal = smooth_planes(padded, planes, kernel)
    partial = signal.reshape(slab_cells, rank)[brain_voxels]
    return reduce_scatter_ta(partial, lax.axis_size("ta"))


def solution(mesh):
    in_specs = (P("gz", None, None, "ta"), P("ta", None), P("gz"))
    out_specs = P(("gz", "ta"), None)
    return jax.shard_map(shards, mesh=mesh, in_specs=in_specs, out_specs=out_specs, check_vma=False)
```

```python
import functools
import math

import jax
import jax.numpy as jnp
from jax import lax
from jax.experimental import pallas as pl
from jax.experimental.pallas import tpu as pltpu
from jax.sharding import PartitionSpec as P

MESH = pl.DeviceIdType.MESH
Z_RING = 16


def kernel_taps():
    sigma = 3.0 / (2.0 * math.sqrt(2.0 * math.log(2.0)))
    raw_taps = [math.exp(-0.5 * (shift_k - 2) ** 2 / sigma**2) for shift_k in range(5)]
    summed = sum(raw_taps)
    return [value_k / summed for value_k in raw_taps]


def smooth_along(source, axis_num, kernel):
    extent = source.shape[axis_num]
    widths = [(0, 0)] * source.ndim
    widths[axis_num] = (2, 2)
    padded = jnp.pad(source, widths)
    summed = jnp.zeros_like(source)
    for shift_k in range(5):
        summed = summed + kernel[shift_k] * lax.slice_in_dim(
            padded, shift_k, shift_k + extent, axis=axis_num
        )
    return summed


def smooth_planes(padded, planes, kernel):
    summed = kernel[0] * padded[0:planes].astype(jnp.float32)
    for shift_k in range(1, 5):
        summed = summed + kernel[shift_k] * padded[shift_k : shift_k + planes].astype(jnp.float32)
    return summed


def rs_kernel(nz, parts, p_ref, o_ref, recv, send, fin, xrecv, send_sem, recv_sem, credit, xsem):
    gz = lax.axis_index("gz")
    ta = lax.axis_index("ta")
    xl = ta // nz
    zi = ta % nz
    right = xl * nz + (zi + 1) % nz
    left = xl * nz + (zi + nz - 1) % nz
    partner = (1 - xl) * nz + zi
    rk = recv.shape[3]

    barrier = pltpu.get_barrier_semaphore()
    for peer in (left, right, partner):
        pl.semaphore_signal(barrier, 1, device_id=(gz, peer), device_id_type=MESH)
    pl.semaphore_wait(barrier, 3)

    dirs = (
        (0, right, left, lambda s: (zi + 2 * nz - s - 1) % nz),
        (1, left, right, lambda s: nz + (zi + s + 1) % nz),
    )
    copies = {}
    for s in range(nz):
        for k in range(parts):
            for d, dst, src_peer, chunk in dirs:
                blk = chunk(s)
                own = p_ref.at[blk, pl.ds(k * rk, rk)]
                if s == 0:
                    src = own
                else:
                    copies[(d, k, s - 1)].wait_recv()
                    val = recv[d, k, (s - 1) % 2] + own[...]
                    if s < nz - 1:
                        if s >= 2:
                            copies[(d, k, s - 2)].wait_send()
                        send[d, k, s % 2] = val
                        src = send.at[d, k, s % 2]
                        if s <= nz - 3:
                            pl.semaphore_signal(
                                credit.at[d, k], 1, device_id=(gz, src_peer), device_id_type=MESH
                            )
                    else:
                        fin[d, pl.ds(k * rk, rk)] = val
                if s < nz - 1:
                    if s >= 2:
                        pl.semaphore_wait(credit.at[d, k], 1)
                    cp = pltpu.make_async_remote_copy(
                        src_ref=src,
                        dst_ref=recv.at[d, k, s % 2],
                        send_sem=send_sem.at[d, k, s % 2],
                        recv_sem=recv_sem.at[d, k, s % 2],
                        device_id=(gz, dst),
                        device_id_type=MESH,
                    )
                    cp.start()
                    copies[(d, k, s)] = cp
            if s == nz - 1:
                xcp = pltpu.make_async_remote_copy(
                    src_ref=fin.at[1 - xl, pl.ds(k * rk, rk)],
                    dst_ref=xrecv.at[pl.ds(k * rk, rk)],
                    send_sem=xsem.at[0, k],
                    recv_sem=xsem.at[1, k],
                    device_id=(gz, partner),
                    device_id_type=MESH,
                )
                xcp.start()
                copies[("x", k)] = xcp

    for d in range(2):
        for k in range(parts):
            for s in (nz - 3, nz - 2):
                copies[(d, k, s)].wait_send()
    for k in range(parts):
        copies[("x", k)].wait_recv()
    o_ref[...] = fin[xl] + xrecv[...]
    for k in range(parts):
        copies[("x", k)].wait_send()


def reduce_scatter_ta(partial, n_ta, parts=14):
    rows_all, cols = partial.shape
    nz = Z_RING
    assert n_ta == 2 * nz
    rows = rows_all // n_ta
    rk = rows // parts
    blocks = partial.reshape(n_ta, rows, cols)
    return pl.pallas_call(
        functools.partial(rs_kernel, nz, parts),
        out_shape=jax.ShapeDtypeStruct((rows, cols), jnp.float32),
        in_specs=[pl.BlockSpec(memory_space=pltpu.VMEM)],
        out_specs=pl.BlockSpec(memory_space=pltpu.VMEM),
        scratch_shapes=[
            pltpu.VMEM((2, parts, 2, rk, cols), jnp.float32),
            pltpu.VMEM((2, parts, 2, rk, cols), jnp.float32),
            pltpu.VMEM((2, rows, cols), jnp.float32),
            pltpu.VMEM((rows, cols), jnp.float32),
            pltpu.SemaphoreType.DMA((2, parts, 2)),
            pltpu.SemaphoreType.DMA((2, parts, 2)),
            pltpu.SemaphoreType.REGULAR((2, parts)),
            pltpu.SemaphoreType.DMA((2, parts)),
        ],
        compiler_params=pltpu.CompilerParams(collective_id=0, has_side_effects=True),
    )(blocks)


def exchange_halo(shard, axis, width):
    peers, length = lax.axis_size(axis), shard.shape[0]
    up = [(i, i + 1) for i in range(peers - 1)]
    down = [(j, i) for i, j in up]
    below = lax.ppermute(shard[length - width :], axis, up)
    above = lax.ppermute(shard[:width], axis, down)
    return below, above


def project_smooth_xy(planes_bf16, sketch_matrix, kernel):
    count, width_x, width_y, time_local = planes_bf16.shape
    projected = jnp.dot(
        planes_bf16.reshape(-1, time_local), sketch_matrix, preferred_element_type=jnp.float32
    ).reshape(count, width_x, width_y, sketch_matrix.shape[1])
    return smooth_along(smooth_along(projected, 1, kernel), 2, kernel)


def shards(volume, sketch_matrix, brain_voxels):
    kernel = kernel_taps()
    planes, width_x, width_y, time_local = volume.shape
    slab_cells = planes * width_x * width_y
    rank = sketch_matrix.shape[1]
    below, above = exchange_halo(volume, "gz", 2)
    local = project_smooth_xy(volume, sketch_matrix, kernel)
    halo = project_smooth_xy(jnp.concatenate([below, above]), sketch_matrix, kernel)
    sources = [halo[0], halo[1]] + [local[p] for p in range(planes)] + [halo[2], halo[3]]
    signal = jnp.stack(
        [sum(kernel[k] * sources[p + k] for k in range(5)) for p in range(planes)]
    )
    partial = signal.reshape(slab_cells, rank)[brain_voxels]
    return reduce_scatter_ta(partial, lax.axis_size("ta"))


def solution(mesh):
    in_specs = (P("gz", None, None, "ta"), P("ta", None), P("gz"))
    out_specs = P(("gz", "ta"), None)
    return jax.shard_map(shards, mesh=mesh, in_specs=in_specs, out_specs=out_specs, check_vma=False)
```

```python
import functools
import math

import jax
import jax.numpy as jnp
from jax import lax
from jax.experimental import pallas as pl
from jax.experimental.pallas import tpu as pltpu
from jax.sharding import PartitionSpec as P

MESH = pl.DeviceIdType.MESH
Z_RING = 16


def kernel_taps():
    sigma = 3.0 / (2.0 * math.sqrt(2.0 * math.log(2.0)))
    raw_taps = [math.exp(-0.5 * (shift_k - 2) ** 2 / sigma**2) for shift_k in range(5)]
    summed = sum(raw_taps)
    return [value_k / summed for value_k in raw_taps]


def smooth_along(source, axis_num, kernel):
    extent = source.shape[axis_num]
    widths = [(0, 0)] * source.ndim
    widths[axis_num] = (2, 2)
    padded = jnp.pad(source, widths)
    summed = jnp.zeros_like(source)
    for shift_k in range(5):
        summed = summed + kernel[shift_k] * lax.slice_in_dim(
            padded, shift_k, shift_k + extent, axis=axis_num
        )
    return summed


def smooth_planes(padded, planes, kernel):
    summed = kernel[0] * padded[0:planes].astype(jnp.float32)
    for shift_k in range(1, 5):
        summed = summed + kernel[shift_k] * padded[shift_k : shift_k + planes].astype(jnp.float32)
    return summed


def rs_kernel(nz, parts, p_ref, o_ref, recv, send, fin, xrecv, send_sem, recv_sem, credit, xsem):
    gz = lax.axis_index("gz")
    ta = lax.axis_index("ta")
    xl = ta // nz
    zi = ta % nz
    right = xl * nz + (zi + 1) % nz
    left = xl * nz + (zi + nz - 1) % nz
    partner = (1 - xl) * nz + zi
    rk = recv.shape[3]

    barrier = pltpu.get_barrier_semaphore()
    for peer in (left, right, partner):
        pl.semaphore_signal(barrier, 1, device_id=(gz, peer), device_id_type=MESH)
    pl.semaphore_wait(barrier, 3)

    dirs = (
        (0, right, left, lambda s: (zi + 2 * nz - s - 1) % nz),
        (1, left, right, lambda s: nz + (zi + s + 1) % nz),
    )
    copies = {}
    for s in range(nz):
        for d, dst, src_peer, chunk in dirs:
            for k in range(parts):
                blk = chunk(s)
                own = p_ref.at[blk, pl.ds(k * rk, rk)]
                if s == 0:
                    src = own
                else:
                    copies[(d, k, s - 1)].wait_recv()
                    val = recv[d, k, (s - 1) % 2] + own[...]
                    if s < nz - 1:
                        if s >= 2:
                            copies[(d, k, s - 2)].wait_send()
                        send[d, k, s % 2] = val
                        src = send.at[d, k, s % 2]
                        if s <= nz - 3:
                            pl.semaphore_signal(
                                credit.at[d, k], 1, device_id=(gz, src_peer), device_id_type=MESH
                            )
                    else:
                        fin[d, pl.ds(k * rk, rk)] = val
                if s < nz - 1:
                    if s >= 2:
                        pl.semaphore_wait(credit.at[d, k], 1)
                    cp = pltpu.make_async_remote_copy(
                        src_ref=src,
                        dst_ref=recv.at[d, k, s % 2],
                        send_sem=send_sem.at[d, k, s % 2],
                        recv_sem=recv_sem.at[d, k, s % 2],
                        device_id=(gz, dst),
                        device_id_type=MESH,
                    )
                    cp.start()
                    copies[(d, k, s)] = cp
        if s == nz - 1:
            for k in range(parts):
                xcp = pltpu.make_async_remote_copy(
                    src_ref=fin.at[1 - xl, pl.ds(k * rk, rk)],
                    dst_ref=xrecv.at[pl.ds(k * rk, rk)],
                    send_sem=xsem.at[0, k],
                    recv_sem=xsem.at[1, k],
                    device_id=(gz, partner),
                    device_id_type=MESH,
                )
                xcp.start()
                copies[("x", k)] = xcp

    for d in range(2):
        for k in range(parts):
            for s in (nz - 3, nz - 2):
                copies[(d, k, s)].wait_send()
    for k in range(parts):
        copies[("x", k)].wait_recv()
    o_ref[...] = fin[xl] + xrecv[...]
    for k in range(parts):
        copies[("x", k)].wait_send()


def reduce_scatter_ta(partial, n_ta, parts=14):
    rows_all, cols = partial.shape
    nz = Z_RING
    assert n_ta == 2 * nz
    rows = rows_all // n_ta
    rk = rows // parts
    blocks = partial.reshape(n_ta, rows, cols)
    return pl.pallas_call(
        functools.partial(rs_kernel, nz, parts),
        out_shape=jax.ShapeDtypeStruct((rows, cols), jnp.float32),
        in_specs=[pl.BlockSpec(memory_space=pltpu.VMEM)],
        out_specs=pl.BlockSpec(memory_space=pltpu.VMEM),
        scratch_shapes=[
            pltpu.VMEM((2, parts, 2, rk, cols), jnp.float32),
            pltpu.VMEM((2, parts, 2, rk, cols), jnp.float32),
            pltpu.VMEM((2, rows, cols), jnp.float32),
            pltpu.VMEM((rows, cols), jnp.float32),
            pltpu.SemaphoreType.DMA((2, parts, 2)),
            pltpu.SemaphoreType.DMA((2, parts, 2)),
            pltpu.SemaphoreType.REGULAR((2, parts)),
            pltpu.SemaphoreType.DMA((2, parts)),
        ],
        compiler_params=pltpu.CompilerParams(collective_id=0, has_side_effects=True),
    )(blocks)


def exchange_halo(shard, axis, width):
    peers, length = lax.axis_size(axis), shard.shape[0]
    up = [(i, i + 1) for i in range(peers - 1)]
    down = [(j, i) for i, j in up]
    below = lax.ppermute(shard[length - width :], axis, up)
    above = lax.ppermute(shard[:width], axis, down)
    return below, above


def project_smooth_xy(planes_bf16, sketch_matrix, kernel):
    count, width_x, width_y, time_local = planes_bf16.shape
    projected = jnp.dot(
        planes_bf16.reshape(-1, time_local), sketch_matrix, preferred_element_type=jnp.float32
    ).reshape(count, width_x, width_y, sketch_matrix.shape[1])
    return smooth_along(smooth_along(projected, 1, kernel), 2, kernel)


def shards(volume, sketch_matrix, brain_voxels):
    kernel = kernel_taps()
    planes, width_x, width_y, time_local = volume.shape
    slab_cells = planes * width_x * width_y
    rank = sketch_matrix.shape[1]
    below, above = exchange_halo(volume, "gz", 2)
    local = project_smooth_xy(volume, sketch_matrix, kernel)
    halo = project_smooth_xy(jnp.concatenate([below, above]), sketch_matrix, kernel)
    padded = jnp.concatenate([halo[:2], local, halo[2:]])
    signal = smooth_planes(padded, planes, kernel)
    partial = signal.reshape(slab_cells, rank)[brain_voxels]
    return reduce_scatter_ta(partial, lax.axis_size("ta"))


def solution(mesh):
    in_specs = (P("gz", None, None, "ta"), P("ta", None), P("gz"))
    out_specs = P(("gz", "ta"), None)
    return jax.shard_map(shards, mesh=mesh, in_specs=in_specs, out_specs=out_specs, check_vma=False)
```

```python
import functools
import math

import jax
import jax.numpy as jnp
from jax import lax
from jax.experimental import pallas as pl
from jax.experimental.pallas import tpu as pltpu
from jax.sharding import PartitionSpec as P

MESH = pl.DeviceIdType.MESH
Z_RING = 16


def kernel_taps():
    sigma = 3.0 / (2.0 * math.sqrt(2.0 * math.log(2.0)))
    raw_taps = [math.exp(-0.5 * (shift_k - 2) ** 2 / sigma**2) for shift_k in range(5)]
    summed = sum(raw_taps)
    return [value_k / summed for value_k in raw_taps]


def smooth_along(source, axis_num, kernel):
    extent = source.shape[axis_num]
    widths = [(0, 0)] * source.ndim
    widths[axis_num] = (2, 2)
    padded = jnp.pad(source, widths)
    summed = jnp.zeros_like(source)
    for shift_k in range(5):
        summed = summed + kernel[shift_k] * lax.slice_in_dim(
            padded, shift_k, shift_k + extent, axis=axis_num
        )
    return summed


def smooth_planes(padded, planes, kernel):
    summed = kernel[0] * padded[0:planes].astype(jnp.float32)
    for shift_k in range(1, 5):
        summed = summed + kernel[shift_k] * padded[shift_k : shift_k + planes].astype(jnp.float32)
    return summed


def rs_kernel(nz, parts, p_ref, o_ref, recv, send, fin, xrecv, send_sem, recv_sem, credit, xsem):
    gz = lax.axis_index("gz")
    ta = lax.axis_index("ta")
    xl = ta // nz
    zi = ta % nz
    right = xl * nz + (zi + 1) % nz
    left = xl * nz + (zi + nz - 1) % nz
    partner = (1 - xl) * nz + zi
    rk = recv.shape[3]

    barrier = pltpu.get_barrier_semaphore()
    for peer in (left, right, partner):
        pl.semaphore_signal(barrier, 1, device_id=(gz, peer), device_id_type=MESH)
    pl.semaphore_wait(barrier, 3)

    dirs = (
        (0, right, left, lambda s: (zi + 2 * nz - s - 1) % nz),
        (1, left, right, lambda s: nz + (zi + s + 1) % nz),
    )
    copies = {}
    for s in range(nz):
        for k in range(parts):
            for d, dst, src_peer, chunk in dirs:
                blk = chunk(s)
                own = p_ref.at[blk, pl.ds(k * rk, rk)]
                if s == 0:
                    src = own
                else:
                    copies[(d, k, s - 1)].wait_recv()
                    val = recv[d, k, (s - 1) % 2] + own[...]
                    if s < nz - 1:
                        if s >= 2:
                            copies[(d, k, s - 2)].wait_send()
                        send[d, k, s % 2] = val
                        src = send.at[d, k, s % 2]
                        if s <= nz - 3:
                            pl.semaphore_signal(
                                credit.at[d, k], 1, device_id=(gz, src_peer), device_id_type=MESH
                            )
                    else:
                        fin[d, pl.ds(k * rk, rk)] = val
                if s < nz - 1:
                    if s >= 2:
                        pl.semaphore_wait(credit.at[d, k], 1)
                    cp = pltpu.make_async_remote_copy(
                        src_ref=src,
                        dst_ref=recv.at[d, k, s % 2],
                        send_sem=send_sem.at[d, k, s % 2],
                        recv_sem=recv_sem.at[d, k, s % 2],
                        device_id=(gz, dst),
                        device_id_type=MESH,
                    )
                    cp.start()
                    copies[(d, k, s)] = cp
            if s == nz - 1:
                xcp = pltpu.make_async_remote_copy(
                    src_ref=fin.at[1 - xl, pl.ds(k * rk, rk)],
                    dst_ref=xrecv.at[pl.ds(k * rk, rk)],
                    send_sem=xsem.at[0, k],
                    recv_sem=xsem.at[1, k],
                    device_id=(gz, partner),
                    device_id_type=MESH,
                )
                xcp.start()
                copies[("x", k)] = xcp

    for d in range(2):
        for k in range(parts):
            for s in (nz - 3, nz - 2):
                copies[(d, k, s)].wait_send()
    for k in range(parts):
        copies[("x", k)].wait_recv()
    o_ref[...] = fin[xl] + xrecv[...]
    for k in range(parts):
        copies[("x", k)].wait_send()


def reduce_scatter_ta(partial, n_ta, parts=14):
    rows_all, cols = partial.shape
    nz = Z_RING
    assert n_ta == 2 * nz
    rows = rows_all // n_ta
    rk = rows // parts
    blocks = partial.reshape(n_ta, rows, cols)
    return pl.pallas_call(
        functools.partial(rs_kernel, nz, parts),
        out_shape=jax.ShapeDtypeStruct((rows, cols), jnp.float32),
        in_specs=[pl.BlockSpec(memory_space=pltpu.VMEM)],
        out_specs=pl.BlockSpec(memory_space=pltpu.VMEM),
        scratch_shapes=[
            pltpu.VMEM((2, parts, 2, rk, cols), jnp.float32),
            pltpu.VMEM((2, parts, 2, rk, cols), jnp.float32),
            pltpu.VMEM((2, rows, cols), jnp.float32),
            pltpu.VMEM((rows, cols), jnp.float32),
            pltpu.SemaphoreType.DMA((2, parts, 2)),
            pltpu.SemaphoreType.DMA((2, parts, 2)),
            pltpu.SemaphoreType.REGULAR((2, parts)),
            pltpu.SemaphoreType.DMA((2, parts)),
        ],
        compiler_params=pltpu.CompilerParams(collective_id=0, has_side_effects=True),
    )(blocks)


def exchange_halo(shard, axis, width):
    peers, length = lax.axis_size(axis), shard.shape[0]
    up = [(i, i + 1) for i in range(peers - 1)]
    down = [(j, i) for i, j in up]
    below = lax.ppermute(shard[length - width :], axis, up)
    above = lax.ppermute(shard[:width], axis, down)
    return below, above


def project_smooth_xy(planes_bf16, sketch_matrix, kernel):
    count, width_x, width_y, time_local = planes_bf16.shape
    projected = jnp.dot(
        planes_bf16.reshape(-1, time_local), sketch_matrix, preferred_element_type=jnp.float32
    ).reshape(count, width_x, width_y, sketch_matrix.shape[1])
    return smooth_along(smooth_along(projected, 1, kernel), 2, kernel)


def shards(volume, sketch_matrix, brain_voxels):
    kernel = kernel_taps()
    planes, width_x, width_y, time_local = volume.shape
    slab_cells = planes * width_x * width_y
    rank = sketch_matrix.shape[1]
    below, above = exchange_halo(volume, "gz", 2)
    local = project_smooth_xy(volume, sketch_matrix, kernel)
    zero = jnp.zeros((2,) + local.shape[1:], local.dtype)
    signal = smooth_planes(jnp.concatenate([zero, local, zero]), planes, kernel)
    halo = project_smooth_xy(jnp.concatenate([below, above]), sketch_matrix, kernel)
    signal = signal.at[0].add(kernel[0] * halo[0] + kernel[1] * halo[1])
    signal = signal.at[1].add(kernel[0] * halo[1])
    signal = signal.at[planes - 2].add(kernel[4] * halo[2])
    signal = signal.at[planes - 1].add(kernel[3] * halo[2] + kernel[4] * halo[3])
    partial = signal.reshape(slab_cells, rank)[brain_voxels]
    return reduce_scatter_ta(partial, lax.axis_size("ta"))


def solution(mesh):
    in_specs = (P("gz", None, None, "ta"), P("ta", None), P("gz"))
    out_specs = P(("gz", "ta"), None)
    return jax.shard_map(shards, mesh=mesh, in_specs=in_specs, out_specs=out_specs, check_vma=False)
```

```python
import functools
import math

import jax
import jax.numpy as jnp
from jax import lax
from jax.experimental import pallas as pl
from jax.experimental.pallas import tpu as pltpu
from jax.sharding import PartitionSpec as P

MESH = pl.DeviceIdType.MESH
Z_RING = 16


def kernel_taps():
    sigma = 3.0 / (2.0 * math.sqrt(2.0 * math.log(2.0)))
    raw_taps = [math.exp(-0.5 * (shift_k - 2) ** 2 / sigma**2) for shift_k in range(5)]
    summed = sum(raw_taps)
    return [value_k / summed for value_k in raw_taps]


def smooth_along(source, axis_num, kernel):
    extent = source.shape[axis_num]
    widths = [(0, 0)] * source.ndim
    widths[axis_num] = (2, 2)
    padded = jnp.pad(source, widths)
    summed = jnp.zeros_like(source)
    for shift_k in range(5):
        summed = summed + kernel[shift_k] * lax.slice_in_dim(
            padded, shift_k, shift_k + extent, axis=axis_num
        )
    return summed


def smooth_planes(padded, planes, kernel):
    summed = kernel[0] * padded[0:planes].astype(jnp.float32)
    for shift_k in range(1, 5):
        summed = summed + kernel[shift_k] * padded[shift_k : shift_k + planes].astype(jnp.float32)
    return summed


def rs_kernel(nz, parts, p_ref, o_ref, recv, send, fin, xrecv, send_sem, recv_sem, credit, xsem):
    gz = lax.axis_index("gz")
    ta = lax.axis_index("ta")
    xl = ta // nz
    zi = ta % nz
    right = xl * nz + (zi + 1) % nz
    left = xl * nz + (zi + nz - 1) % nz
    partner = (1 - xl) * nz + zi
    rk = recv.shape[3]

    barrier = pltpu.get_barrier_semaphore()
    for peer in (left, right, partner):
        pl.semaphore_signal(barrier, 1, device_id=(gz, peer), device_id_type=MESH)
    pl.semaphore_wait(barrier, 3)

    dirs = (
        (0, right, left, lambda s: (zi + 2 * nz - s - 1) % nz),
        (1, left, right, lambda s: nz + (zi + s + 1) % nz),
    )
    copies = {}
    for s in range(nz):
        for k in range(parts):
            for d, dst, src_peer, chunk in dirs:
                blk = chunk(s)
                own = p_ref.at[blk, pl.ds(k * rk, rk)]
                if s == 0:
                    src = own
                else:
                    copies[(d, k, s - 1)].wait_recv()
                    val = recv[d, k, (s - 1) % 2] + own[...]
                    if s < nz - 1:
                        if s >= 2:
                            copies[(d, k, s - 2)].wait_send()
                        send[d, k, s % 2] = val
                        src = send.at[d, k, s % 2]
                        if s <= nz - 3:
                            pl.semaphore_signal(
                                credit.at[d, k], 1, device_id=(gz, src_peer), device_id_type=MESH
                            )
                    else:
                        fin[d, pl.ds(k * rk, rk)] = val
                if s < nz - 1:
                    if s >= 2:
                        pl.semaphore_wait(credit.at[d, k], 1)
                    cp = pltpu.make_async_remote_copy(
                        src_ref=src,
                        dst_ref=recv.at[d, k, s % 2],
                        send_sem=send_sem.at[d, k, s % 2],
                        recv_sem=recv_sem.at[d, k, s % 2],
                        device_id=(gz, dst),
                        device_id_type=MESH,
                    )
                    cp.start()
                    copies[(d, k, s)] = cp
            if s == nz - 1:
                xcp = pltpu.make_async_remote_copy(
                    src_ref=fin.at[1 - xl, pl.ds(k * rk, rk)],
                    dst_ref=xrecv.at[pl.ds(k * rk, rk)],
                    send_sem=xsem.at[0, k],
                    recv_sem=xsem.at[1, k],
                    device_id=(gz, partner),
                    device_id_type=MESH,
                )
                xcp.start()
                copies[("x", k)] = xcp

    for d in range(2):
        for k in range(parts):
            for s in (nz - 3, nz - 2):
                copies[(d, k, s)].wait_send()
    for k in range(parts):
        copies[("x", k)].wait_recv()
    o_ref[...] = fin[xl] + xrecv[...]
    for k in range(parts):
        copies[("x", k)].wait_send()


def reduce_scatter_ta(partial, n_ta, parts=14):
    rows_all, cols = partial.shape
    nz = Z_RING
    assert n_ta == 2 * nz
    rows = rows_all // n_ta
    rk = rows // parts
    blocks = partial.reshape(n_ta, rows, cols)
    return pl.pallas_call(
        functools.partial(rs_kernel, nz, parts),
        out_shape=jax.ShapeDtypeStruct((rows, cols), jnp.float32),
        in_specs=[pl.BlockSpec(memory_space=pltpu.VMEM)],
        out_specs=pl.BlockSpec(memory_space=pltpu.VMEM),
        scratch_shapes=[
            pltpu.VMEM((2, parts, 2, rk, cols), jnp.float32),
            pltpu.VMEM((2, parts, 2, rk, cols), jnp.float32),
            pltpu.VMEM((2, rows, cols), jnp.float32),
            pltpu.VMEM((rows, cols), jnp.float32),
            pltpu.SemaphoreType.DMA((2, parts, 2)),
            pltpu.SemaphoreType.DMA((2, parts, 2)),
            pltpu.SemaphoreType.REGULAR((2, parts)),
            pltpu.SemaphoreType.DMA((2, parts)),
        ],
        compiler_params=pltpu.CompilerParams(collective_id=0, has_side_effects=True),
    )(blocks)


def exchange_halo(shard, axis, width):
    peers, length = lax.axis_size(axis), shard.shape[0]
    up = [(i, i + 1) for i in range(peers - 1)]
    down = [(j, i) for i, j in up]
    below = lax.ppermute(shard[length - width :], axis, up)
    above = lax.ppermute(shard[:width], axis, down)
    return below, above


def project_smooth_xy(planes_bf16, sketch_matrix, kernel):
    count, width_x, width_y, time_local = planes_bf16.shape
    projected = jnp.dot(
        planes_bf16.reshape(-1, time_local), sketch_matrix, preferred_element_type=jnp.float32
    ).reshape(count, width_x, width_y, sketch_matrix.shape[1])
    return smooth_along(smooth_along(projected, 1, kernel), 2, kernel)


def shards(volume, sketch_matrix, brain_voxels):
    kernel = kernel_taps()
    planes, width_x, width_y, time_local = volume.shape
    slab_cells = planes * width_x * width_y
    rank = sketch_matrix.shape[1]
    below, above = exchange_halo(volume, "gz", 2)
    local = project_smooth_xy(volume, sketch_matrix, kernel)
    lower = project_smooth_xy(below, sketch_matrix, kernel)
    upper = project_smooth_xy(above, sketch_matrix, kernel)
    padded = jnp.concatenate([lower, local, upper])
    signal = smooth_planes(padded, planes, kernel)
    partial = signal.reshape(slab_cells, rank)[brain_voxels]
    return reduce_scatter_ta(partial, lax.axis_size("ta"))


def solution(mesh):
    in_specs = (P("gz", None, None, "ta"), P("ta", None), P("gz"))
    out_specs = P(("gz", "ta"), None)
    return jax.shard_map(shards, mesh=mesh, in_specs=in_specs, out_specs=out_specs, check_vma=False)
```

```python
import functools
import math

import jax
import jax.numpy as jnp
from jax import lax
from jax.experimental import pallas as pl
from jax.experimental.pallas import tpu as pltpu
from jax.sharding import PartitionSpec as P

MESH = pl.DeviceIdType.MESH
Z_RING = 16


def kernel_taps():
    sigma = 3.0 / (2.0 * math.sqrt(2.0 * math.log(2.0)))
    raw_taps = [math.exp(-0.5 * (shift_k - 2) ** 2 / sigma**2) for shift_k in range(5)]
    summed = sum(raw_taps)
    return [value_k / summed for value_k in raw_taps]


def smooth_along(source, axis_num, kernel):
    extent = source.shape[axis_num]
    widths = [(0, 0)] * source.ndim
    widths[axis_num] = (2, 2)
    padded = jnp.pad(source, widths)
    summed = jnp.zeros_like(source)
    for shift_k in range(5):
        summed = summed + kernel[shift_k] * lax.slice_in_dim(
            padded, shift_k, shift_k + extent, axis=axis_num
        )
    return summed


def smooth_planes(padded, planes, kernel):
    summed = kernel[0] * padded[0:planes].astype(jnp.float32)
    for shift_k in range(1, 5):
        summed = summed + kernel[shift_k] * padded[shift_k : shift_k + planes].astype(jnp.float32)
    return summed


def rs_kernel(nz, parts, p_ref, o_ref, recv, send, fin, xrecv, send_sem, recv_sem, credit, xsem):
    gz = lax.axis_index("gz")
    ta = lax.axis_index("ta")
    xl = ta // nz
    zi = ta % nz
    right = xl * nz + (zi + 1) % nz
    left = xl * nz + (zi + nz - 1) % nz
    partner = (1 - xl) * nz + zi
    rk = recv.shape[3]

    barrier = pltpu.get_barrier_semaphore()
    for peer in (left, right, partner):
        pl.semaphore_signal(barrier, 1, device_id=(gz, peer), device_id_type=MESH)
    pl.semaphore_wait(barrier, 3)

    dirs = (
        (0, right, left, lambda s: (zi + 2 * nz - s - 1) % nz),
        (1, left, right, lambda s: nz + (zi + s + 1) % nz),
    )
    copies = {}
    for s in range(nz):
        for k in range(parts):
            for d, dst, src_peer, chunk in dirs:
                blk = chunk(s)
                own = p_ref.at[blk, pl.ds(k * rk, rk)]
                if s == 0:
                    src = own
                else:
                    copies[(d, k, s - 1)].wait_recv()
                    val = recv[d, k, (s - 1) % 2] + own[...]
                    if s < nz - 1:
                        if s >= 2:
                            copies[(d, k, s - 2)].wait_send()
                        send[d, k, s % 2] = val
                        src = send.at[d, k, s % 2]
                        if s <= nz - 3:
                            pl.semaphore_signal(
                                credit.at[d, k], 1, device_id=(gz, src_peer), device_id_type=MESH
                            )
                    else:
                        fin[d, pl.ds(k * rk, rk)] = val
                if s < nz - 1:
                    if s >= 2:
                        pl.semaphore_wait(credit.at[d, k], 1)
                    cp = pltpu.make_async_remote_copy(
                        src_ref=src,
                        dst_ref=recv.at[d, k, s % 2],
                        send_sem=send_sem.at[d, k, s % 2],
                        recv_sem=recv_sem.at[d, k, s % 2],
                        device_id=(gz, dst),
                        device_id_type=MESH,
                    )
                    cp.start()
                    copies[(d, k, s)] = cp
            if s == nz - 1:
                xcp = pltpu.make_async_remote_copy(
                    src_ref=fin.at[1 - xl, pl.ds(k * rk, rk)],
                    dst_ref=xrecv.at[pl.ds(k * rk, rk)],
                    send_sem=xsem.at[0, k],
                    recv_sem=xsem.at[1, k],
                    device_id=(gz, partner),
                    device_id_type=MESH,
                )
                xcp.start()
                copies[("x", k)] = xcp

    for d in range(2):
        for k in range(parts):
            for s in (nz - 3, nz - 2):
                copies[(d, k, s)].wait_send()
    for k in range(parts):
        copies[("x", k)].wait_recv()
    o_ref[...] = fin[xl] + xrecv[...]
    for k in range(parts):
        copies[("x", k)].wait_send()


def reduce_scatter_ta(partial, n_ta, parts=14):
    rows_all, cols = partial.shape
    nz = Z_RING
    assert n_ta == 2 * nz
    rows = rows_all // n_ta
    rk = rows // parts
    blocks = partial.reshape(n_ta, rows, cols)
    return pl.pallas_call(
        functools.partial(rs_kernel, nz, parts),
        out_shape=jax.ShapeDtypeStruct((rows, cols), jnp.float32),
        in_specs=[pl.BlockSpec(memory_space=pltpu.VMEM)],
        out_specs=pl.BlockSpec(memory_space=pltpu.VMEM),
        scratch_shapes=[
            pltpu.VMEM((2, parts, 2, rk, cols), jnp.float32),
            pltpu.VMEM((2, parts, 2, rk, cols), jnp.float32),
            pltpu.VMEM((2, rows, cols), jnp.float32),
            pltpu.VMEM((rows, cols), jnp.float32),
            pltpu.SemaphoreType.DMA((2, parts, 2)),
            pltpu.SemaphoreType.DMA((2, parts, 2)),
            pltpu.SemaphoreType.REGULAR((2, parts)),
            pltpu.SemaphoreType.DMA((2, parts)),
        ],
        compiler_params=pltpu.CompilerParams(collective_id=0, has_side_effects=True),
    )(blocks)


def exchange_halo(shard, axis, width):
    peers, length = lax.axis_size(axis), shard.shape[0]
    up = [(i, i + 1) for i in range(peers - 1)]
    down = [(j, i) for i, j in up]
    below = lax.ppermute(shard[length - width :], axis, up)
    above = lax.ppermute(shard[:width], axis, down)
    return below, above


def project_smooth_xy(planes_bf16, sketch_matrix, kernel):
    count, width_x, width_y, time_local = planes_bf16.shape
    projected = jnp.dot(
        planes_bf16.reshape(-1, time_local), sketch_matrix, preferred_element_type=jnp.float32
    ).reshape(count, width_x, width_y, sketch_matrix.shape[1])
    return smooth_along(smooth_along(projected, 1, kernel), 2, kernel)


def shards(volume, sketch_matrix, brain_voxels):
    kernel = kernel_taps()
    planes, width_x, width_y, time_local = volume.shape
    slab_cells = planes * width_x * width_y
    rank = sketch_matrix.shape[1]
    below, above = exchange_halo(volume, "gz", 2)
    local = project_smooth_xy(volume, sketch_matrix, kernel)
    lower = project_smooth_xy(below, sketch_matrix, kernel)
    upper = project_smooth_xy(above, sketch_matrix, kernel)
    early = smooth_planes(jnp.concatenate([lower, local]), planes - 2, kernel)
    late = smooth_planes(jnp.concatenate([local[2:], upper]), 2, kernel)
    signal = jnp.concatenate([early, late])
    partial = signal.reshape(slab_cells, rank)[brain_voxels]
    return reduce_scatter_ta(partial, lax.axis_size("ta"))


def solution(mesh):
    in_specs = (P("gz", None, None, "ta"), P("ta", None), P("gz"))
    out_specs = P(("gz", "ta"), None)
    return jax.shard_map(shards, mesh=mesh, in_specs=in_specs, out_specs=out_specs, check_vma=False)
```
